512 devices in a mesh: leaf: 32 (over x, z_lo, core), col: 16 (over y, z_hi).
Axes of the slice: x: 4, y: 4, z: 16 (z_hi: 4, z_lo: 4; z = z_hi * 4 + z_lo), core: 2. Of those that a mesh axis runs over, the one named last changes fastest.
Arguments:
- right_sides: float32 [256, 65536], P('col', 'leaf'), may hold values from -6 to 6
- inverse_first: float32 [128, 128, 128], P('leaf'), may hold values from -0.5 to 0.5
- coupling_first: float32 [128, 3, 128, 128], P('leaf'), may hold values from -0.3125 to 0.3125
- links_first: int32 [128, 3], P('leaf'), may hold values from 0 to 11, as said below
- order_first: int32 [32, 12], P('leaf'), may hold values from 0 to 11, as said below
- inverse_second: float32 [128, 128, 128], P('leaf'), may hold values from -0.5 to 0.5
- coupling_second: float32 [128, 3, 128, 128], P('leaf'), may hold values from -0.3125 to 0.3125
- links_second: int32 [128, 3], P('leaf'), may hold values from 0 to 7, as said below
- order_second: int32 [32, 8], P('leaf'), may hold values from 0 to 7, as said below
- inverse_third: float32 [128, 128, 128], P('leaf'), may hold values from -0.5 to 0.5
- coupling_third: float32 [128, 3, 128, 128], P('leaf'), may hold values from -0.3125 to 0.3125
- links_third: int32 [128, 3], P('leaf'), may hold values from 0 to 3, as said below
- order_third: int32 [32, 4], P('leaf'), may hold values from 0 to 3, as said below
- front_rows: int32 [3, 32], P(None, 'leaf'), may hold values from 128 to 512
- root_inverse: float32 [2, 8192, 8192], P(None, 'leaf', 'col'), may hold values from -0.0625 to 0.0625
- root_coupling: float32 [8192, 8192], P('leaf', 'col'), may hold values from -0.0625 to 0.0625
Outputs:
- solved_first: float32 [256, 16384], P('col', 'leaf')
- solved_second: float32 [256, 16384], P('col', 'leaf')
- solved_third: float32 [256, 16384], P('col', 'leaf')
- root_solution: float32 [256, 2, 8192], P('col', None, 'leaf')
The draws below stay inside these ranges and needn't reach their ends.
Inputs may be any that keep to these rules, and one draw needn't show every extreme that they name: `links_first`: each row names 3 different skeleton blocks of its front. `links_second`: each row names 3 different skeleton blocks of its front. `links_third`: each row names 3 different skeleton blocks of its front. `order_first`: each row is a permutation. `order_second`: each row is a permutation. `order_third`: each row is a permutation.
All inputs are finite; a program needn't handle non-finite values.
Results may differ from the reference program's by a relative error of at most 0.0003.
Values sent between devices are 32-bit elements; how exact they have to be, the bound alone decides.
A program may use at most 64 MiB of HBM per device.

```python
import jax
import jax.numpy as jnp
from jax import lax

BLK = 128
RED = 4
NSK = 3
SKEL2 = 4
LEVELS = 3
NPAN = 2
NRHS = 256
SKEL1 = 8
SKEL0 = 12
SECTION0 = 16
FRONTS = 32
PANEL_ROWS = 256
PANEL = 8192


def pick_links(key, row_total, choice_total):
    scores = jax.random.randint(key, (row_total, choice_total), 0, 65536) * choice_total + jnp.arange(choice_total, dtype=jnp.int32)[None, :]
    ranking = jnp.argsort(scores, axis=1)
    return ranking[:, :NSK].astype(jnp.int32)


def pick_orders(key, choice_total):
    scores = jax.random.randint(key, (FRONTS, choice_total), 0, 65536) * choice_total + jnp.arange(choice_total, dtype=jnp.int32)[None, :]
    return jnp.argsort(scores, axis=1).astype(jnp.int32)


def draw_links_first(key, part):
    return pick_links(jax.random.fold_in(key, 11), FRONTS * RED, SKEL0)


def draw_links_second(key, part):
    return pick_links(jax.random.fold_in(key, 12), FRONTS * RED, SKEL1)


def draw_links_third(key, part):
    return pick_links(jax.random.fold_in(key, 13), FRONTS * RED, SKEL2)


def draw_order_first(key, part):
    return pick_orders(jax.random.fold_in(key, 21), SKEL0)


def draw_order_second(key, part):
    return pick_orders(jax.random.fold_in(key, 22), SKEL1)


def draw_order_third(key, part):
    return pick_orders(jax.random.fold_in(key, 23), SKEL2)


def draw_front_rows(key, part):
    largest_rows = RED * BLK
    fewest_rows = largest_rows // 4
    values = jax.random.randint(jax.random.fold_in(key, 31), (LEVELS, FRONTS), fewest_rows, largest_rows + 1)
    chosen_fronts = jax.random.randint(jax.random.fold_in(key, 32), (LEVELS,), 0, FRONTS)
    front_slots = jnp.arange(FRONTS, dtype=jnp.int32)[None, :]
    values = jnp.where(front_slots == chosen_fronts[:, None], largest_rows, values)
    values = jnp.where(front_slots == (chosen_fronts[:, None] + 1) % FRONTS, fewest_rows, values)
    return values.astype(jnp.int32)


def steps_of(stream_key, shape, cuts, low, top_value):
    factor_of, own = 1.0, jax.random.fold_in(stream_key, 6)
    for axis_at, blocks in cuts:
        heights = jnp.exp(jax.random.uniform(jax.random.fold_in(own, axis_at), (blocks,), jnp.float32, low / len(cuts), top_value / len(cuts)))
        factor_of = factor_of * jnp.repeat(heights, shape[axis_at] // blocks).reshape([-1 if axis == axis_at else 1 for axis in range(len(shape))])
    return factor_of


def centred(own_key, dims, width, bound, cuts=(), kind=jnp.bfloat16):
    result = width * jax.random.normal(own_key, dims, jnp.float32)
    if cuts:
        result = result * steps_of(own_key, dims, cuts, -0.22, 0.18)
    return jnp.clip(result, -bound, bound).astype(kind)


def setup_inputs(seed: int = 0) -> dict:
    arg_keys = jax.random.split(jax.random.key(seed), 17)
    return {
        "right_sides": centred(arg_keys[0], (NRHS, FRONTS * SECTION0 * BLK), 1.0, 6.0, ((0, 16), (1, 32)), jnp.float32),
        "inverse_first": centred(arg_keys[1], (FRONTS * RED, BLK, BLK), BLK ** -0.5, 0.5, ((0, 32),), jnp.float32),
        "coupling_first": centred(arg_keys[2], (FRONTS * RED, NSK, BLK, BLK), (NSK * BLK) ** -0.5, 0.3125, ((0, 32),), jnp.float32),
        "links_first": draw_links_first(jax.random.fold_in(arg_keys[16], 71), 0),
        "order_first": draw_order_first(jax.random.fold_in(arg_keys[16], 71), 0),
        "inverse_second": centred(arg_keys[5], (FRONTS * RED, BLK, BLK), BLK ** -0.5, 0.5, ((0, 32),), jnp.float32),
        "coupling_second": centred(arg_keys[6], (FRONTS * RED, NSK, BLK, BLK), (NSK * BLK) ** -0.5, 0.3125, ((0, 32),), jnp.float32),
        "links_second": draw_links_second(jax.random.fold_in(arg_keys[16], 71), 0),
        "order_second": draw_order_second(jax.random.fold_in(arg_keys[16], 71), 0),
        "inverse_third": centred(arg_keys[9], (FRONTS * RED, BLK, BLK), BLK ** -0.5, 0.5, ((0, 32),), jnp.float32),
        "coupling_third": centred(arg_keys[10], (FRONTS * RED, NSK, BLK, BLK), (NSK * BLK) ** -0.5, 0.3125, ((0, 32),), jnp.float32),
        "links_third": draw_links_third(jax.random.fold_in(arg_keys[16], 71), 0),
        "order_third": draw_order_third(jax.random.fold_in(arg_keys[16], 71), 0),
        "front_rows": draw_front_rows(jax.random.fold_in(arg_keys[16], 71), 0),
        "root_inverse": centred(arg_keys[14], (NPAN, PANEL, PANEL), PANEL ** -0.5, 0.0625, ((1, 32), (2, 16)), jnp.float32),
        "root_coupling": centred(arg_keys[15], (PANEL, PANEL), PANEL ** -0.5, 0.0625, ((0, 32), (1, 16)), jnp.float32),
    }


def product(left_side, right_side):
    return jnp.dot(left_side, right_side, precision=lax.Precision.HIGHEST, preferred_element_type=jnp.float32)


def eliminate(section, inverse, coupling, link_ids, live_count):
    skeleton_count = section.shape[2] - RED
    positions = jnp.arange(RED, dtype=jnp.int32)[:, None] * BLK + jnp.arange(BLK, dtype=jnp.int32)[None, :]
    live_rows = (positions[None, :, :] < live_count[:, None, None]).astype(jnp.float32)
    redundant = section[:, :, :RED] * live_rows[None]
    solved = jnp.einsum("rfib,fiba->rfia", redundant, inverse, precision=lax.Precision.HIGHEST) * live_rows[None]
    pushed = jnp.einsum("rfia,fikab->rfikb", solved, coupling, precision=lax.Precision.HIGHEST)
    targets = (link_ids[:, :, :, None] == jnp.arange(skeleton_count, dtype=jnp.int32)).astype(jnp.float32)
    update = jnp.einsum("rfikb,fiks->rfsb", pushed, targets, precision=lax.Precision.HIGHEST)
    return solved, section[:, :, RED:] - update


def join_halves(skeleton, level_index):
    half_blocks = skeleton.shape[2] // 2
    fronts_all = jnp.arange(FRONTS, dtype=jnp.int32)
    upper_half = (fronts_all >> level_index) & 1
    lower_front = fronts_all - upper_half * (2 ** level_index)
    upper_front = lower_front + 2 ** level_index
    split = skeleton.reshape(skeleton.shape[0], FRONTS, 2, half_blocks, BLK)
    first_part = split[:, lower_front, upper_half]
    second_part = split[:, upper_front, upper_half]
    return jnp.concatenate([first_part, second_part], 2)


def reference(right_sides, inverse_first, coupling_first, links_first, order_first, inverse_second, coupling_second, links_second, order_second, inverse_third, coupling_third, links_third, order_third, front_rows, root_inverse, root_coupling):
    section = right_sides.reshape(NRHS, FRONTS, SECTION0, BLK)
    level_data = ((inverse_first, coupling_first, links_first, order_first), (inverse_second, coupling_second, links_second, order_second), (inverse_third, coupling_third, links_third, order_third))
    outputs = []
    for level_index in range(3):
        inverse, coupling, link_ids, order_map = level_data[level_index]
        solved, skeleton = eliminate(section, inverse.reshape(FRONTS, RED, BLK, BLK), coupling.reshape(FRONTS, RED, NSK, BLK, BLK), link_ids.reshape(FRONTS, RED, NSK), front_rows[level_index])
        outputs.append(solved.reshape(NRHS, FRONTS * RED * BLK))
        if level_index < 2:
            skeleton = join_halves(skeleton, level_index)
        section = jnp.take_along_axis(skeleton, order_map[None, :, :, None], axis=2)
    root_rhs = section.reshape(NRHS, FRONTS, NPAN, PANEL_ROWS).transpose(0, 2, 1, 3).reshape(NRHS, NPAN, PANEL)
    first_solve = product(root_rhs[:, 0], root_inverse[0])
    coupled = product(first_solve, root_coupling)
    second_solve = product(root_rhs[:, 1] - coupled, root_inverse[1])
    last_panel = product(second_solve, root_inverse[1].T)
    back_coupled = product(last_panel, root_coupling.T)
    first_panel = product(first_solve - back_coupled, root_inverse[0].T)
    root_solution = jnp.stack([first_panel, last_panel], 1)
    return (outputs[0], outputs[1], outputs[2], root_solution)
```

```python
import jax
import jax.numpy as jnp
from jax import lax
from jax.experimental import pallas as pl
from jax.experimental.pallas import tpu as pltpu
from jax.sharding import PartitionSpec as P

MESH = pl.DeviceIdType.MESH
SIDE = 4
ROWS = 8
GROUPS = SIDE * SIDE
TOTAL = GROUPS * ROWS
HALF = 256
SPAN = 512
STEPS = 6
MESSAGES = 96


def partner(block, axis, stride):
    count = lax.axis_size(axis)
    route = []
    for low in range(count):
        high = low | 1 << stride
        if high != low and high < count:
            route += [(low, high), (high, low)]
    return lax.ppermute(block, axis, route)


def eliminate(section, inverse, coupling, link_ids, live_count):
    block_rows = inverse.shape[-1]
    red_blocks = inverse.shape[0]
    link_total = coupling.shape[1]
    rhs_rows = section.shape[0]
    skeleton_count = section.shape[1] // block_rows - red_blocks
    redundant = section[:, : red_blocks * block_rows].reshape(rhs_rows, red_blocks, block_rows)
    positions = lax.broadcasted_iota(
        jnp.int32, (red_blocks, block_rows), 0
    ) * block_rows + lax.broadcasted_iota(jnp.int32, (red_blocks, block_rows), 1)
    live_rows = (positions < live_count).astype(jnp.float32)
    solved = (
        jnp.einsum("rib,iba->ria", redundant * live_rows, inverse, precision=lax.Precision.HIGHEST)
        * live_rows
    )
    pushed = jnp.einsum("ria,ikab->rikb", solved, coupling, precision=lax.Precision.HIGHEST)
    targets = (
        link_ids[:, :, None]
        == lax.broadcasted_iota(jnp.int32, (red_blocks, link_total, skeleton_count), 2)
    ).astype(jnp.float32)
    update = jnp.einsum("rikb,iks->rsb", pushed, targets, precision=lax.Precision.HIGHEST)
    skeleton = (
        section[:, red_blocks * block_rows :].reshape(rhs_rows, skeleton_count, block_rows) - update
    )
    return (solved.reshape(rhs_rows, red_blocks * block_rows), skeleton)


def join_halves(skeleton, level_index):
    half_blocks = skeleton.shape[1] // 2
    upper_half = lax.axis_index("leaf") >> level_index & 1
    kept_half = lax.dynamic_slice_in_dim(skeleton, upper_half * half_blocks, half_blocks, 1)
    sent_half = lax.dynamic_slice_in_dim(skeleton, (1 - upper_half) * half_blocks, half_blocks, 1)
    received = partner(sent_half, "leaf", level_index)
    return jnp.where(
        upper_half == 0,
        jnp.concatenate([kept_half, received], 1),
        jnp.concatenate([received, kept_half], 1),
    )


def device(x, z_lo, core, y, z_hi):
    return (x * (2 * SIDE) + z_lo * 2 + core, y * SIDE + z_hi)


def root_kernel(
    section,
    inverse,
    coupling,
    out,
    own,
    sibling,
    high,
    low,
    pieces,
    turned,
    gathered,
    partial,
    first_in,
    first_sum,
    second_in,
    solved,
    final_in,
    send_sem,
    recv_sem,
    local_sem,
):
    leaf, col = lax.axis_index("leaf"), lax.axis_index("col")
    x, z_lo, core = leaf // (2 * SIDE), leaf // 2 % SIDE, leaf % 2
    y, z_hi = col // SIDE, col % SIDE
    chip_row = leaf // 2
    other = 1 - core
    same = jnp.logical_and(x == y, z_lo == z_hi)

    def around(axis, step):
        at = {"x": x, "z_lo": z_lo, "y": y, "z_hi": z_hi}
        at[axis] = lax.rem(at[axis] + step, SIDE)
        return device(at["x"], at["z_lo"], core, at["y"], at["z_hi"])

    twin = device(x, z_lo, other, y, z_hi)
    turn_forward = [device(y, z_hi, core, x, k) for k in range(SIDE)]
    turn_backward = [device(y, k, core, x, z_lo) for k in range(SIDE)]

    barrier = pltpu.get_barrier_semaphore()
    pl.semaphore_signal(barrier, inc=1, device_id=twin, device_id_type=MESH)
    for axis in ("x", "z_lo", "y", "z_hi"):
        for step in range(1, SIDE):
            pl.semaphore_signal(barrier, inc=1, device_id=around(axis, step), device_id_type=MESH)
    for targets, mine in ((turn_forward, z_hi), (turn_backward, z_lo)):
        for k in range(SIDE):
            itself = jnp.logical_and(same, mine == k)

            @pl.when(jnp.logical_not(itself))
            def _():
                pl.semaphore_signal(barrier, inc=1, device_id=targets[k], device_id_type=MESH)

    loads = []
    for k in range(3):
        source = coupling if k == 1 else inverse.at[k // 2]
        loads.append(pltpu.make_async_copy(source, own.at[k], local_sem.at[k]))
        loads[-1].start()
    pl.semaphore_wait(barrier, 1 + 4 * (SIDE - 1) + 2 * SIDE - 2 * same.astype(jnp.int32))

    used = [0]
    pending = []

    def take(count):
        used[0] += count
        return used[0] - count

    def send(source, target, to):
        n = take(1)
        copy = pltpu.make_async_remote_copy(
            src_ref=source,
            dst_ref=target,
            send_sem=send_sem.at[n],
            recv_sem=recv_sem.at[n],
            device_id=to,
            device_id_type=MESH,
        )
        copy.start()
        pending.append(copy.wait_send)
        return copy

    def send_unless_same(source, target, to, itself, sent, received):
        remote = pltpu.make_async_remote_copy(
            src_ref=source,
            dst_ref=target,
            send_sem=send_sem.at[sent],
            recv_sem=recv_sem.at[received],
            device_id=to,
            device_id_type=MESH,
        )

        @pl.when(jnp.logical_not(itself))
        def _():
            remote.start()

        @pl.when(itself)
        def _():
            pltpu.make_async_copy(source, target, recv_sem.at[received]).start()

        def finish():
            @pl.when(jnp.logical_not(itself))
            def _():
                remote.wait_send()

        pending.append(finish)
        return remote

    mine_at = pl.multiple_of(core * HALF, HALF)
    other_at = pl.multiple_of(other * HALF, HALF)
    kept = pl.ds(pl.multiple_of(core * ROWS, ROWS), ROWS)
    given = pl.ds(pl.multiple_of(other * ROWS, ROWS), ROWS)
    swaps = [
        send(
            section.at[given, pl.ds(p * HALF, HALF)],
            pieces.at[p, :, pl.ds(mine_at, HALF)],
            twin,
        )
        for p in range(2)
    ]
    factors = [
        send(coupling if k == 1 else inverse.at[k // 2], sibling.at[k], twin) for k in range(3)
    ]
    for p in range(2):
        pieces[p, :, pl.ds(mine_at, HALF)] = section[kept, p * HALF : (p + 1) * HALF]

    def rows_of(group):
        return pl.ds(pl.multiple_of(group * ROWS, ROWS), ROWS)

    def band_of(member):
        return pl.ds(pl.multiple_of(member * SIDE * ROWS, SIDE * ROWS), SIDE * ROWS)

    def gather_second(step, axis, member):
        band = gathered.at[step, band_of(member)]
        copies = [send(band, band, around(axis, d)) for d in (2, 1, 3)]
        return copies

    def gather_plain(step, piece, group, near, far, member):
        target = gathered.at[step, rows_of(group)]
        copies = [send(piece, target, around(near, d)) for d in (2, 1, 3)]
        gathered[step, rows_of(group)] = piece[...]
        for copy in copies:
            copy.wait_recv()
        return gather_second(step, far, member)

    def gather_turned(step, piece, group, targets, mine, slot, far, member):
        target = gathered.at[step, rows_of(group)]
        base = take(SIDE)
        for k in range(SIDE):
            send_unless_same(
                piece,
                target,
                targets[k],
                jnp.logical_and(same, mine == k),
                base + k,
                base + slot,
            )
        for k in range(SIDE):
            pltpu.make_async_remote_copy(
                src_ref=piece,
                dst_ref=target,
                send_sem=send_sem.at[base + k],
                recv_sem=recv_sem.at[base + k],
                device_id=twin,
                device_id_type=MESH,
            ).wait_recv()
        return gather_second(step, far, member)

    def split(k):
        for source, at in ((own, mine_at), (sibling, other_at)):
            if source is own:
                loads[k].wait()
            else:
                factors[k].wait_recv()
            value = source[k]
            top = value.astype(jnp.bfloat16)
            high[k, pl.ds(at, HALF), :] = top
            low[k, pl.ds(at, HALF), :] = (value - top.astype(jnp.float32)).astype(jnp.bfloat16)

    def multiply(step, k, transposed):
        value = gathered[step]
        top = value.astype(jnp.bfloat16)
        rest = (value - top.astype(jnp.float32)).astype(jnp.bfloat16)
        both = jnp.concatenate([top, rest], 0)
        for half in range(2):
            cut = slice(half * HALF, (half + 1) * HALF)
            if transposed:
                right_high, right_low = high[k, cut, :], low[k, cut, :]
            else:
                right_high, right_low = high[k, :, cut], low[k, :, cut]
            dims = (((1,), (1 if transposed else 0,)), ((), ()))
            wide = lax.dot_general(both, right_high, dims, preferred_element_type=jnp.float32)
            thin = lax.dot_general(top, right_low, dims, preferred_element_type=jnp.float32)
            partial[step, :, cut] = wide[:TOTAL] + (wide[TOTAL:] + thin)

    def reduce(step, far, near, far_at, near_at, meanwhile=None):
        copies = []
        for d in (2, 1, 3):
            to = lax.rem(far_at + d, SIDE)
            copies.append(
                send(partial.at[step, band_of(to)], first_in.at[step, d - 1], around(far, d))
            )
        if meanwhile is not None:
            meanwhile()
        for copy in copies:
            copy.wait_recv()
        total = partial[step, band_of(far_at)]
        first_sum[step] = total + first_in[step, 0] + (first_in[step, 1] + first_in[step, 2])
        copies = []
        for d in (2, 1, 3):
            to = lax.rem(near_at + d, SIDE)
            copies.append(
                send(first_sum.at[step, rows_of(to)], second_in.at[step, d - 1], around(near, d))
            )
        for copy in copies:
            copy.wait_recv()
        total = first_sum[step, rows_of(near_at)]
        return total + second_in[step, 0] + (second_in[step, 1] + second_in[step, 2])

    def wait_all(copies):
        for copy in copies:
            copy.wait_recv()

    def give_result(step, panel):
        copy = send(
            solved.at[step, :, pl.ds(other_at, HALF)], final_in.at[panel], twin
        )
        out[kept, panel * HALF : (panel + 1) * HALF] = solved[step, :, pl.ds(mine_at, HALF)]
        return copy

    def take_result(copy, panel):
        copy.wait_recv()
        out[given, panel * HALF : (panel + 1) * HALF] = final_in[panel]

    swaps[0].wait_recv()
    copies = gather_plain(0, pieces.at[0], col, "z_hi", "y", y)
    swaps[1].wait_recv()
    n = take(1)
    turning = send_unless_same(
        pieces.at[1], turned, device(y, z_hi, core, x, z_lo), same, n, n
    )
    split(0)
    wait_all(copies)

    multiply(0, 0, False)
    solved[0] = reduce(0, "x", "z_lo", x, z_lo, lambda: split(1))
    copies = gather_turned(1, solved.at[0], chip_row, turn_forward, z_hi, z_lo, "y", y)
    wait_all(copies)

    multiply(1, 1, False)
    total = reduce(1, "x", "z_lo", x, z_lo, lambda: split(2))
    turning.wait_recv()
    solved[1] = turned[...] - total
    copies = gather_turned(2, solved.at[1], chip_row, turn_forward, z_hi, z_lo, "y", y)
    wait_all(copies)

    multiply(2, 2, False)
    solved[2] = reduce(2, "x", "z_lo", x, z_lo)
    copies = gather_plain(3, solved.at[2], chip_row, "z_lo", "x", x)
    wait_all(copies)

    multiply(3, 2, True)
    solved[3] = reduce(3, "y", "z_hi", y, z_hi)
    copies = gather_turned(4, solved.at[3], col, turn_backward, z_lo, z_hi, "x", x)
    last = give_result(3, 1)
    wait_all(copies)

    multiply(4, 1, True)
    total = reduce(4, "y", "z_hi", y, z_hi)
    solved[4] = gathered[1, rows_of(col)] - total
    copies = gather_turned(5, solved.at[4], col, turn_backward, z_lo, z_hi, "x", x)
    wait_all(copies)

    multiply(5, 0, True)
    solved[5] = reduce(5, "y", "z_hi", y, z_hi)
    first = give_result(5, 0)
    take_result(last, 1)
    take_result(first, 0)
    for finish in pending:
        finish()


def root_solve(section, root_inverse, root_coupling):
    f32, bf16 = jnp.float32, jnp.bfloat16
    return pl.pallas_call(
        root_kernel,
        out_shape=jax.ShapeDtypeStruct((2 * ROWS, 2 * HALF), f32),
        in_specs=[
            pl.BlockSpec(memory_space=pltpu.VMEM),
            pl.BlockSpec(memory_space=pl.ANY),
            pl.BlockSpec(memory_space=pl.ANY),
        ],
        out_specs=pl.BlockSpec(memory_space=pltpu.VMEM),
        scratch_shapes=[
            pltpu.VMEM((3, HALF, SPAN), f32),
            pltpu.VMEM((3, HALF, SPAN), f32),
            pltpu.VMEM((3, SPAN, SPAN), bf16),
            pltpu.VMEM((3, SPAN, SPAN), bf16),
            pltpu.VMEM((2, ROWS, SPAN), f32),
            pltpu.VMEM((ROWS, SPAN), f32),
            pltpu.VMEM((STEPS, TOTAL, SPAN), f32),
            pltpu.VMEM((STEPS, TOTAL, SPAN), f32),
            pltpu.VMEM((STEPS, SIDE - 1, SIDE * ROWS, SPAN), f32),
            pltpu.VMEM((STEPS, SIDE * ROWS, SPAN), f32),
            pltpu.VMEM((STEPS, SIDE - 1, ROWS, SPAN), f32),
            pltpu.VMEM((STEPS, ROWS, SPAN), f32),
            pltpu.VMEM((2, ROWS, HALF), f32),
            pltpu.SemaphoreType.DMA((MESSAGES,)),
            pltpu.SemaphoreType.DMA((MESSAGES,)),
            pltpu.SemaphoreType.DMA((3,)),
        ],
        compiler_params=pltpu.CompilerParams(
            collective_id=0, has_side_effects=True, vmem_limit_bytes=40 << 20
        ),
        name="root_solve",
    )(section, root_inverse, root_coupling)


def local(
    right_sides,
    inverse_first,
    coupling_first,
    links_first,
    order_first,
    inverse_second,
    coupling_second,
    links_second,
    order_second,
    inverse_third,
    coupling_third,
    links_third,
    order_third,
    front_rows,
    root_inverse,
    root_coupling,
):
    level_data = (
        (inverse_first, coupling_first, links_first, order_first),
        (inverse_second, coupling_second, links_second, order_second),
        (inverse_third, coupling_third, links_third, order_third),
    )
    section = right_sides
    outputs = []
    for level_index in range(3):
        inverse, coupling, link_ids, order_map = level_data[level_index]
        solved, skeleton = eliminate(
            section, inverse, coupling, link_ids, front_rows[level_index, 0]
        )
        outputs.append(solved)
        if level_index < 2:
            skeleton = join_halves(skeleton, level_index)
        skeleton = jnp.take(skeleton, order_map[0], axis=1)
        section = skeleton.reshape(skeleton.shape[0], -1)
    root_solution = root_solve(section, root_inverse, root_coupling)
    rhs_rows = right_sides.shape[0]
    return (*outputs, root_solution.reshape(rhs_rows, 2, HALF))


def solution(mesh):
    in_specs = (
        P("col", "leaf"),
        P("leaf", None, None),
        P("leaf", None, None, None),
        P("leaf", None),
        P("leaf", None),
        P("leaf", None, None),
        P("leaf", None, None, None),
        P("leaf", None),
        P("leaf", None),
        P("leaf", None, None),
        P("leaf", None, None, None),
        P("leaf", None),
        P("leaf", None),
        P(None, "leaf"),
        P(None, "leaf", "col"),
        P("leaf", "col"),
    )
    out_specs = (P("col", "leaf"), P("col", "leaf"), P("col", "leaf"), P("col", None, "leaf"))
    return jax.shard_map(local, mesh=mesh, in_specs=in_specs, out_specs=out_specs, check_vma=False)
```

```python
import jax
import jax.numpy as jnp
from jax import lax
from jax.experimental import pallas as pl
from jax.experimental.pallas import tpu as pltpu
from jax.sharding import PartitionSpec as P

MESH = pl.DeviceIdType.MESH
SIDE = 4
ROWS = 8
GROUPS = SIDE * SIDE
TOTAL = GROUPS * ROWS
HALF = 256
SPAN = 512
BLOCK = 128
RED = 4
LINKS = 3
SKELETONS = (12, 8, 4)
STEPS = 6
MESSAGES = 160


def device(x, z_lo, core, y, z_hi):
    return (x * (2 * SIDE) + z_lo * 2 + core, y * SIDE + z_hi)


def rows_of(group):
    return pl.ds(pl.multiple_of(group * ROWS, ROWS), ROWS)


def band_of(member):
    return pl.ds(pl.multiple_of(member * SIDE * ROWS, SIDE * ROWS), SIDE * ROWS)


def solve_kernel(
    right_sides,
    inverse_first,
    coupling_first,
    links_first,
    order_first,
    inverse_second,
    coupling_second,
    links_second,
    order_second,
    inverse_third,
    coupling_third,
    links_third,
    order_third,
    front_rows,
    root_inverse,
    root_coupling,
    out_first,
    out_second,
    out_third,
    out,
    first_rows,
    front_inverse,
    front_coupling,
    front_solve,
    front_push,
    updated,
    joined_first,
    joined_second,
    joined_third,
    section,
    own,
    sibling,
    high,
    low,
    pieces,
    turned,
    crossed,
    moved,
    gathered,
    partial,
    leaf_in,
    first_in,
    first_sum,
    second_in,
    quarter,
    solved,
    final_in,
    send_sem,
    recv_sem,
    local_sem,
):
    leaf, col = lax.axis_index("leaf"), lax.axis_index("col")
    x, z_lo, core = leaf // (2 * SIDE), leaf // 2 % SIDE, leaf % 2
    y, z_hi = col // SIDE, col % SIDE
    chip_row = leaf // 2
    other = 1 - core
    same_plane = x == y
    same_depth = z_lo == z_hi

    def around(axis, step):
        at = {"x": x, "z_lo": z_lo, "y": y, "z_hi": z_hi}
        at[axis] = lax.rem(at[axis] + step, SIDE)
        return device(at["x"], at["z_lo"], core, at["y"], at["z_hi"])

    twin = device(x, z_lo, other, y, z_hi)
    neighbour = device(x, z_lo + 1 - 2 * (z_lo % 2), core, y, z_hi)
    sunk = device(x, z_hi, core, y, z_lo)
    flipped = device(y, z_lo, core, x, z_hi)
    leaf_steps = [(a, b) for a in (2, 1, 3, 0) for b in (3, 2, 1, 0) if a or b]
    leaf_targets = [
        device(lax.rem(x + a, SIDE), lax.rem(z_lo + b, SIDE), core, y, z_hi) for a, b in leaf_steps
    ]
    depth_forward = (
        [device(x, z_hi, core, y, k) for k in range(SIDE)],
        [jnp.logical_and(same_depth, z_hi == k) for k in range(SIDE)],
        z_lo,
    )
    depth_backward = (
        [device(x, k, core, y, z_lo) for k in range(SIDE)],
        [jnp.logical_and(same_depth, z_lo == k) for k in range(SIDE)],
        z_hi,
    )
    plane_forward = (
        [device(y, z_lo, core, k, z_hi) for k in range(SIDE)],
        [jnp.logical_and(same_plane, y == k) for k in range(SIDE)],
        x,
    )
    plane_backward = (
        [device(k, z_lo, core, x, z_hi) for k in range(SIDE)],
        [jnp.logical_and(same_plane, x == k) for k in range(SIDE)],
        y,
    )

    front_data = (
        (inverse_first, coupling_first, links_first, order_first, out_first),
        (inverse_second, coupling_second, links_second, order_second, out_second),
        (inverse_third, coupling_third, links_third, order_third, out_third),
    )
    first_load = pltpu.make_async_copy(right_sides, first_rows, local_sem.at[9])
    first_load.start()
    front_loads = []
    for level in range(3):
        pair = (
            pltpu.make_async_copy(
                front_data[level][0], front_inverse.at[level], local_sem.at[2 * level]
            ),
            pltpu.make_async_copy(
                front_data[level][1], front_coupling.at[level], local_sem.at[2 * level + 1]
            ),
        )
        for load in pair:
            load.start()
        front_loads.append(pair)
    factor_of = (root_inverse.at[0], root_coupling, root_inverse.at[1])
    loads = []
    for k in range(3):
        loads.append(pltpu.make_async_copy(factor_of[k], own.at[k], local_sem.at[6 + k]))
        loads[-1].start()

    barrier = pltpu.get_barrier_semaphore()

    def greet(to):
        pl.semaphore_signal(barrier, inc=1, device_id=to, device_id_type=MESH)

    greet(twin)
    for to in leaf_targets:
        greet(to)
    for axis in ("y", "z_hi"):
        for step in range(1, SIDE):
            greet(around(axis, step))
    for targets, itself, _ in (depth_forward, depth_backward, plane_forward, plane_backward):
        for k in range(SIDE):

            @pl.when(jnp.logical_not(itself[k]))
            def _():
                greet(targets[k])

    used = [0]
    pending = []

    def take(count):
        used[0] += count
        return used[0] - count

    def send(source, target, to):
        n = take(1)
        copy = pltpu.make_async_remote_copy(
            src_ref=source,
            dst_ref=target,
            send_sem=send_sem.at[n],
            recv_sem=recv_sem.at[n],
            device_id=to,
            device_id_type=MESH,
        )
        copy.start()
        pending.append(copy.wait_send)
        return copy

    def send_unless_same(source, target, to, itself, sent, received):
        remote = pltpu.make_async_remote_copy(
            src_ref=source,
            dst_ref=target,
            send_sem=send_sem.at[sent],
            recv_sem=recv_sem.at[received],
            device_id=to,
            device_id_type=MESH,
        )

        @pl.when(jnp.logical_not(itself))
        def _():
            remote.start()

        @pl.when(itself)
        def _():
            pltpu.make_async_copy(source, target, recv_sem.at[received]).start()

        def finish():
            @pl.when(jnp.logical_not(itself))
            def _():
                remote.wait_send()

        pending.append(finish)
        return remote

    def flush(count):
        for finish in pending[:count]:
            finish()
        del pending[:count]

    def wait_all(copies):
        for copy in copies:
            copy.wait_recv()

    def turn(source, target, route):
        targets, itself, slot = route
        base = take(SIDE)
        for k in range(SIDE):
            send_unless_same(source, target, targets[k], itself[k], base + k, base + slot)
        return [
            pltpu.make_async_remote_copy(
                src_ref=source,
                dst_ref=target,
                send_sem=send_sem.at[base + k],
                recv_sem=recv_sem.at[base + k],
                device_id=twin,
                device_id_type=MESH,
            )
            for k in range(SIDE)
        ]

    joined = (joined_first, joined_second, joined_third)
    lanes = lax.broadcasted_iota(jnp.int32, (2 * ROWS, BLOCK), 1)

    def halves(value):
        top = value.astype(jnp.bfloat16)
        return top, (value - top.astype(jnp.float32)).astype(jnp.bfloat16)

    def prepare(level):
        for load in front_loads[level]:
            load.wait()
        for i in range(RED):
            parts = [(front_solve, 0, front_inverse[level, i])]
            parts += [(front_push, k, front_coupling[level, i, k]) for k in range(LINKS)]
            for target, k, value in parts:
                top, rest = halves(value)
                cut = slice(k * BLOCK, (k + 1) * BLOCK)
                target[level, i, 0:BLOCK, cut] = top
                target[level, i, BLOCK : 2 * BLOCK, cut] = top
                target[level, i, 2 * BLOCK : 3 * BLOCK, cut] = rest

    def thrice(value, operator):
        top, rest = halves(value)
        return jnp.dot(
            jnp.concatenate([top, rest, top], 1), operator, preferred_element_type=jnp.float32
        )

    def eliminate(level, block_at):
        _, _, links, _, result = front_data[level]
        live_count = front_rows[level, 0]
        values = []
        for i in range(RED):
            live = (lanes + i * BLOCK < live_count).astype(jnp.float32)
            value = live * thrice(live * block_at(i), front_solve[level, i])
            result[:, i * BLOCK : (i + 1) * BLOCK] = value
            values.append(value)
        pushed = []
        for i in range(RED):
            product = thrice(values[i], front_push[level, i])
            for k in range(LINKS):
                pushed.append((links[i, k], product[:, k * BLOCK : (k + 1) * BLOCK]))
        for j in range(SKELETONS[level]):
            update = jnp.zeros((2 * ROWS, BLOCK), jnp.float32)
            for link, product in pushed:
                update += jnp.where(link == j, 1.0, 0.0) * product
            updated[level, j] = block_at(RED + j) - update

    def join(level, half_at, to):
        half = SKELETONS[level] // 2
        copy = send(
            updated.at[level, pl.ds((1 - half_at) * half, half)],
            joined[level].at[pl.ds(half_at * half, half)],
            to,
        )
        for j in range(half):
            joined[level][half_at * half + j] = updated[level, half_at * half + j]
        return copy

    def ordered(level):
        order = front_data[level][3]
        return lambda k: joined[level][order[0, k]]

    prepare(0)
    first_load.wait()
    eliminate(0, lambda k: first_rows[:, k * BLOCK : (k + 1) * BLOCK])
    prepare(1)
    prepare(2)
    pl.semaphore_wait(
        barrier,
        1
        + (GROUPS - 1)
        + 2 * (SIDE - 1)
        + 4 * SIDE
        - 2 * same_plane.astype(jnp.int32)
        - 2 * same_depth.astype(jnp.int32),
    )
    joining = join(0, core, twin)
    factors = [send(factor_of[k], sibling.at[k], twin) for k in range(3)]
    joining.wait_recv()
    eliminate(1, ordered(0))
    joining = join(1, z_lo % 2, neighbour)
    joining.wait_recv()
    eliminate(2, ordered(1))
    for j in range(SKELETONS[2]):
        joined[2][j] = updated[2, j]
    last_block = ordered(2)
    for k in range(SKELETONS[2]):
        section[k // 2, :, k % 2 * BLOCK : (k % 2 + 1) * BLOCK] = last_block(k)

    mine_at = pl.multiple_of(core * HALF, HALF)
    other_at = pl.multiple_of(other * HALF, HALF)
    kept = pl.ds(pl.multiple_of(core * ROWS, ROWS), ROWS)
    given = pl.ds(pl.multiple_of(other * ROWS, ROWS), ROWS)
    swaps = [
        send(section.at[p, given, :], pieces.at[p, :, pl.ds(mine_at, HALF)], twin)
        for p in range(2)
    ]
    for p in range(2):
        pieces[p, :, pl.ds(mine_at, HALF)] = section[p, kept, :]

    def split(k):
        for source, at in ((own, mine_at), (sibling, other_at)):
            if source is own:
                loads[k].wait()
            else:
                factors[k].wait_recv()
            value = source[k]
            high[k, pl.ds(at, HALF), :], low[k, pl.ds(at, HALF), :] = halves(value)

    def multiply(step, k, transposed):
        top, rest = halves(gathered[step])
        both = jnp.concatenate([top, rest], 0)
        for half in range(2):
            cut = slice(half * HALF, (half + 1) * HALF)
            if transposed:
                right_high, right_low = high[k, cut, :], low[k, cut, :]
            else:
                right_high, right_low = high[k, :, cut], low[k, :, cut]
            dims = (((1,), (1 if transposed else 0,)), ((), ()))
            wide = lax.dot_general(both, right_high, dims, preferred_element_type=jnp.float32)
            thin = lax.dot_general(top, right_low, dims, preferred_element_type=jnp.float32)
            partial[step, :, cut] = wide[:TOTAL] + (wide[TOTAL:] + thin)

    def reduce_leaf(step, meanwhile):
        copies = []
        for n, (a, b) in enumerate(leaf_steps):
            group = lax.rem(x + a, SIDE) * SIDE + lax.rem(z_lo + b, SIDE)
            copies.append(
                send(partial.at[step, rows_of(group)], leaf_in.at[step, n], leaf_targets[n])
            )
        flush(len(pending) - len(copies))
        meanwhile()
        wait_all(copies)
        parts = [partial[step, rows_of(chip_row)]] + [leaf_in[step, n] for n in range(len(copies))]
        while len(parts) > 1:
            parts = [sum(parts[i : i + 2][1:], parts[i]) for i in range(0, len(parts), 2)]
        return parts[0]

    def gather_forward(step, piece):
        copies = turn(piece, moved.at[step - 1, rows_of(z_lo)], depth_forward)
        flush(len(pending) - SIDE)
        wait_all(copies)
        copies = turn(moved.at[step - 1], gathered.at[step, band_of(x)], plane_forward)
        flush(len(pending) - SIDE)
        wait_all(copies)

    def reduce_columns(step, meanwhile):
        at = step - 3
        copies = []
        for d in (2, 1, 3):
            to = lax.rem(y + d, SIDE)
            copies.append(
                send(partial.at[step, band_of(to)], first_in.at[at, d - 1], around("y", d))
            )
        flush(len(pending) - len(copies))
        meanwhile()
        wait_all(copies)
        total = partial[step, band_of(y)]
        first_sum[at] = total + first_in[at, 0] + (first_in[at, 1] + first_in[at, 2])

    def reduce_backward(step):
        at = step - 3
        targets, itself, slot = depth_backward
        base = take(SIDE)
        for k in range(SIDE):
            send_unless_same(
                first_sum.at[at, k * ROWS : (k + 1) * ROWS],
                second_in.at[at, slot],
                targets[k],
                itself[k],
                base + k,
                base + slot,
            )
        flush(len(pending) - SIDE)
        for k in range(SIDE):
            pltpu.make_async_remote_copy(
                src_ref=second_in.at[at, k],
                dst_ref=second_in.at[at, k],
                send_sem=send_sem.at[base + k],
                recv_sem=recv_sem.at[base + k],
                device_id=twin,
                device_id_type=MESH,
            ).wait_recv()
        return (second_in[at, 0] + second_in[at, 1]) + (second_in[at, 2] + second_in[at, 3])

    def gather_backward(step, piece, meanwhile):
        at = step - 4
        copies = [
            send(piece, quarter.at[at, rows_of(z_lo)], around("z_lo", d)) for d in (2, 3, 1)
        ]
        quarter[at, rows_of(z_lo)] = piece[...]
        flush(len(pending) - len(copies))
        wait_all(copies)
        copies = turn(quarter.at[at], gathered.at[step, band_of(y)], plane_backward)
        flush(len(pending) - SIDE)
        meanwhile()
        wait_all(copies)

    def give_result(source, panel):
        copy = send(source.at[:, pl.ds(other_at, HALF)], final_in.at[panel], twin)
        out[kept, panel * HALF : (panel + 1) * HALF] = source[:, pl.ds(mine_at, HALF)]
        return copy

    def take_result(copy, panel):
        copy.wait_recv()
        out[given, panel * HALF : (panel + 1) * HALF] = final_in[panel]

    def nothing():
        pass

    wait_all(swaps)
    copies = [
        send(pieces.at[0], gathered.at[0, rows_of(col)], around("z_hi", d)) for d in (2, 1, 3)
    ]
    n = take(1)
    sinking = send_unless_same(pieces.at[1], turned.at[0], sunk, same_depth, n, n)
    gathered[0, rows_of(col)] = pieces[0]
    split(0)
    wait_all(copies)
    band = gathered.at[0, band_of(y)]
    copies = [send(band, band, around("y", d)) for d in (2, 1, 3)]
    flush(len(pending) - len(copies))
    wait_all(copies)

    multiply(0, 0, False)
    solved[0] = reduce_leaf(0, lambda: split(1))
    n = take(1)
    crossing = send_unless_same(solved.at[0], crossed, flipped, same_plane, n, n)
    gather_forward(1, solved.at[0])

    multiply(1, 1, False)
    turning = []

    def turn_on():
        split(2)
        sinking.wait_recv()
        n = take(1)
        turning.append(
            send_unless_same(turned.at[0], turned.at[1], flipped, same_plane, n, n)
        )

    total = reduce_leaf(1, turn_on)
    turning[0].wait_recv()
    solved[1] = turned[1] - total
    gather_forward(2, solved.at[1])

    multiply(2, 2, False)
    solved[2] = reduce_leaf(2, nothing)
    copies = [send(solved.at[2], gathered.at[3, rows_of(chip_row)], to) for to in leaf_targets]
    gathered[3, rows_of(chip_row)] = solved[2]
    flush(len(pending) - len(copies))
    wait_all(copies)

    multiply(3, 2, True)
    reduce_columns(3, nothing)
    solved[3] = reduce_backward(3)
    n = take(1)
    lifting = send_unless_same(solved.at[3], solved.at[4], sunk, same_depth, n, n)
    gather_backward(4, solved.at[3], nothing)

    multiply(4, 1, True)
    reduce_columns(4, nothing)
    total = reduce_backward(4)
    crossing.wait_recv()
    solved[5] = crossed[...] - total
    handed = []

    def hand_last():
        lifting.wait_recv()
        handed.append(give_result(solved.at[4], 1))

    gather_backward(5, solved.at[5], hand_last)

    multiply(5, 0, True)
    reduce_columns(5, nothing)
    copies = []
    for d in (2, 1, 3):
        to = lax.rem(z_hi + d, SIDE)
        copies.append(
            send(first_sum.at[2, rows_of(to)], second_in.at[2, d - 1], around("z_hi", d))
        )
    flush(len(pending) - len(copies))
    take_result(handed[0], 1)
    wait_all(copies)
    total = first_sum[2, rows_of(z_hi)]
    solved[6] = total + second_in[2, 0] + (second_in[2, 1] + second_in[2, 2])
    first = give_result(solved.at[6], 0)
    take_result(first, 0)
    flush(len(pending))


def local(*operands):
    f32, bf16 = jnp.float32, jnp.bfloat16
    rhs_rows = operands[0].shape[0]
    vmem = pl.BlockSpec(memory_space=pltpu.VMEM)
    smem = pl.BlockSpec(memory_space=pltpu.SMEM)
    whole = pl.BlockSpec(memory_space=pltpu.HBM)
    outputs = pl.pallas_call(
        solve_kernel,
        out_shape=[jax.ShapeDtypeStruct((rhs_rows, SPAN), f32)] * 4,
        in_specs=[whole] + [whole, whole, smem, smem] * 3 + [smem, whole, whole],
        out_specs=[vmem] * 4,
        scratch_shapes=[
            pltpu.VMEM((2 * ROWS, GROUPS * BLOCK), f32),
            pltpu.VMEM((3, RED, BLOCK, BLOCK), f32),
            pltpu.VMEM((3, RED, LINKS, BLOCK, BLOCK), f32),
            pltpu.VMEM((3, RED, 3 * BLOCK, BLOCK), bf16),
            pltpu.VMEM((3, RED, 3 * BLOCK, LINKS * BLOCK), bf16),
            pltpu.VMEM((3, SKELETONS[0], 2 * ROWS, BLOCK), f32),
            pltpu.VMEM((SKELETONS[0], 2 * ROWS, BLOCK), f32),
            pltpu.VMEM((SKELETONS[1], 2 * ROWS, BLOCK), f32),
            pltpu.VMEM((SKELETONS[2], 2 * ROWS, BLOCK), f32),
            pltpu.VMEM((2, 2 * ROWS, HALF), f32),
            pltpu.VMEM((3, HALF, SPAN), f32),
            pltpu.VMEM((3, HALF, SPAN), f32),
            pltpu.VMEM((3, SPAN, SPAN), bf16),
            pltpu.VMEM((3, SPAN, SPAN), bf16),
            pltpu.VMEM((2, ROWS, SPAN), f32),
            pltpu.VMEM((2, ROWS, SPAN), f32),
            pltpu.VMEM((ROWS, SPAN), f32),
            pltpu.VMEM((2, SIDE * ROWS, SPAN), f32),
            pltpu.VMEM((STEPS, TOTAL, SPAN), f32),
            pltpu.VMEM((STEPS, TOTAL, SPAN), f32),
            pltpu.VMEM((3, GROUPS - 1, ROWS, SPAN), f32),
            pltpu.VMEM((3, SIDE - 1, SIDE * ROWS, SPAN), f32),
            pltpu.VMEM((3, SIDE * ROWS, SPAN), f32),
            pltpu.VMEM((3, SIDE, ROWS, SPAN), f32),
            pltpu.VMEM((2, SIDE * ROWS, SPAN), f32),
            pltpu.VMEM((7, ROWS, SPAN), f32),
            pltpu.VMEM((2, ROWS, HALF), f32),
            pltpu.SemaphoreType.DMA((MESSAGES,)),
            pltpu.SemaphoreType.DMA((MESSAGES,)),
            pltpu.SemaphoreType.DMA((10,)),
        ],
        compiler_params=pltpu.CompilerParams(
            collective_id=0, has_side_effects=True, vmem_limit_bytes=63 << 20
        ),
        name="solve",
    )(*operands)
    return (*outputs[:3], outputs[3].reshape(rhs_rows, 2, HALF))


def solution(mesh):
    in_specs = (
        P("col", "leaf"),
        P("leaf", None, None),
        P("leaf", None, None, None),
        P("leaf", None),
        P("leaf", None),
        P("leaf", None, None),
        P("leaf", None, None, None),
        P("leaf", None),
        P("leaf", None),
        P("leaf", None, None),
        P("leaf", None, None, None),
        P("leaf", None),
        P("leaf", None),
        P(None, "leaf"),
        P(None, "leaf", "col"),
        P("leaf", "col"),
    )
    out_specs = (P("col", "leaf"), P("col", "leaf"), P("col", "leaf"), P("col", None, "leaf"))
    return jax.shard_map(local, mesh=mesh, in_specs=in_specs, out_specs=out_specs, check_vma=False)
```

```python
import jax
import jax.numpy as jnp
from jax import lax
from jax.experimental import pallas as pl
from jax.experimental.pallas import tpu as pltpu
from jax.sharding import PartitionSpec as P

MESH = pl.DeviceIdType.MESH
SIDE = 4
ROWS = 8
GROUPS = SIDE * SIDE
TOTAL = GROUPS * ROWS
HALF = 256
SPAN = 512
BLOCK = 128
RED = 4
LINKS = 3
SKELETONS = (12, 8, 4)
STEPS = 6
MESSAGES = 160


def device(x, z_lo, core, y, z_hi):
    return (x * (2 * SIDE) + z_lo * 2 + core, y * SIDE + z_hi)


def rows_of(group):
    return pl.ds(pl.multiple_of(group * ROWS, ROWS), ROWS)


def band_of(member):
    return pl.ds(pl.multiple_of(member * SIDE * ROWS, SIDE * ROWS), SIDE * ROWS)


def solve_kernel(
    right_sides,
    inverse_first,
    coupling_first,
    links_first,
    order_first,
    inverse_second,
    coupling_second,
    links_second,
    order_second,
    inverse_third,
    coupling_third,
    links_third,
    order_third,
    front_rows,
    root_inverse,
    root_coupling,
    out_first,
    out_second,
    out_third,
    out,
    first_rows,
    front_inverse,
    front_coupling,
    front_solve,
    front_push,
    updated,
    joined_first,
    joined_second,
    joined_third,
    section,
    own,
    sibling,
    high,
    low,
    pieces,
    turned,
    crossed,
    moved,
    gathered,
    partial,
    leaf_in,
    first_in,
    first_sum,
    second_in,
    solved,
    final_in,
    send_sem,
    recv_sem,
    local_sem,
):
    leaf, col = lax.axis_index("leaf"), lax.axis_index("col")
    x, z_lo, core = leaf // (2 * SIDE), leaf // 2 % SIDE, leaf % 2
    y, z_hi = col // SIDE, col % SIDE
    chip_row = leaf // 2
    other = 1 - core
    same_plane = x == y
    same_depth = z_lo == z_hi

    def around(axis, step):
        at = {"x": x, "z_lo": z_lo, "y": y, "z_hi": z_hi}
        at[axis] = lax.rem(at[axis] + step, SIDE)
        return device(at["x"], at["z_lo"], core, at["y"], at["z_hi"])

    twin = device(x, z_lo, other, y, z_hi)
    neighbour = device(x, z_lo + 1 - 2 * (z_lo % 2), core, y, z_hi)
    sunk = device(x, z_hi, core, y, z_lo)
    flipped = device(y, z_lo, core, x, z_hi)
    leaf_steps = [(a, b) for a in (2, 1, 3, 0) for b in (3, 2, 1, 0) if a or b]
    leaf_targets = [
        device(lax.rem(x + a, SIDE), lax.rem(z_lo + b, SIDE), core, y, z_hi) for a, b in leaf_steps
    ]
    depth_forward = (
        [device(x, z_hi, core, y, k) for k in range(SIDE)],
        [jnp.logical_and(same_depth, z_hi == k) for k in range(SIDE)],
        z_lo,
    )
    depth_backward = (
        [device(x, k, core, y, z_lo) for k in range(SIDE)],
        [jnp.logical_and(same_depth, z_lo == k) for k in range(SIDE)],
        z_hi,
    )
    plane_forward = (
        [device(y, z_lo, core, k, z_hi) for k in range(SIDE)],
        [jnp.logical_and(same_plane, y == k) for k in range(SIDE)],
        x,
    )
    plane_backward = (
        [device(k, z_lo, core, x, z_hi) for k in range(SIDE)],
        [jnp.logical_and(same_plane, x == k) for k in range(SIDE)],
        y,
    )

    front_data = (
        (inverse_first, coupling_first, links_first, order_first, out_first),
        (inverse_second, coupling_second, links_second, order_second, out_second),
        (inverse_third, coupling_third, links_third, order_third, out_third),
    )
    first_load = pltpu.make_async_copy(right_sides, first_rows, local_sem.at[9])
    first_load.start()
    front_loads = []
    for level in range(3):
        pair = (
            pltpu.make_async_copy(
                front_data[level][0], front_inverse.at[level], local_sem.at[2 * level]
            ),
            pltpu.make_async_copy(
                front_data[level][1], front_coupling.at[level], local_sem.at[2 * level + 1]
            ),
        )
        for load in pair:
            load.start()
        front_loads.append(pair)
    factor_of = (root_inverse.at[0], root_coupling, root_inverse.at[1])
    loads = []
    for k in range(3):
        loads.append(pltpu.make_async_copy(factor_of[k], own.at[k], local_sem.at[6 + k]))
        loads[-1].start()

    barrier = pltpu.get_barrier_semaphore()

    def greet(to):
        pl.semaphore_signal(barrier, inc=1, device_id=to, device_id_type=MESH)

    for targets, itself, _ in (depth_forward, depth_backward, plane_forward, plane_backward):
        for k in range(SIDE):

            @pl.when(jnp.logical_not(itself[k]))
            def _():
                greet(targets[k])

    for axis in ("z_hi", "y"):
        for step in (2, 1, 3):
            greet(around(axis, step))
    for to in leaf_targets:
        greet(to)
    greet(twin)

    def meet():
        pl.semaphore_wait(
            barrier,
            1
            + (GROUPS - 1)
            + 2 * (SIDE - 1)
            + 4 * SIDE
            - 2 * same_plane.astype(jnp.int32)
            - 2 * same_depth.astype(jnp.int32),
        )

    used = [0]
    pending = []

    def take(count):
        used[0] += count
        return used[0] - count

    def send(source, target, to):
        n = take(1)
        copy = pltpu.make_async_remote_copy(
            src_ref=source,
            dst_ref=target,
            send_sem=send_sem.at[n],
            recv_sem=recv_sem.at[n],
            device_id=to,
            device_id_type=MESH,
        )
        copy.start()
        pending.append(copy.wait_send)
        return copy

    def send_unless_same(source, target, to, itself, sent, received):
        remote = pltpu.make_async_remote_copy(
            src_ref=source,
            dst_ref=target,
            send_sem=send_sem.at[sent],
            recv_sem=recv_sem.at[received],
            device_id=to,
            device_id_type=MESH,
        )

        @pl.when(jnp.logical_not(itself))
        def _():
            remote.start()

        @pl.when(itself)
        def _():
            pltpu.make_async_copy(source, target, recv_sem.at[received]).start()

        def finish():
            @pl.when(jnp.logical_not(itself))
            def _():
                remote.wait_send()

        pending.append(finish)
        return remote

    def flush(count):
        for finish in pending[:count]:
            finish()
        del pending[:count]

    def wait_all(copies):
        for copy in copies:
            copy.wait_recv()

    def turn(source, target, route):
        targets, itself, slot = route
        base = take(SIDE)
        for k in range(SIDE):
            send_unless_same(source, target, targets[k], itself[k], base + k, base + slot)
        return [
            pltpu.make_async_remote_copy(
                src_ref=source,
                dst_ref=target,
                send_sem=send_sem.at[base + k],
                recv_sem=recv_sem.at[base + k],
                device_id=twin,
                device_id_type=MESH,
            )
            for k in range(SIDE)
        ]

    joined = (joined_first, joined_second, joined_third)
    lanes = lax.broadcasted_iota(jnp.int32, (2 * ROWS, BLOCK), 1)

    def halves(value):
        top = value.astype(jnp.bfloat16)
        return top, (value - top.astype(jnp.float32)).astype(jnp.bfloat16)

    def prepare(level):
        for load in front_loads[level]:
            load.wait()
        for i in range(RED):
            parts = [(front_solve, 0, front_inverse[level, i])]
            parts += [(front_push, k, front_coupling[level, i, k]) for k in range(LINKS)]
            for target, k, value in parts:
                top, rest = halves(value)
                cut = slice(k * BLOCK, (k + 1) * BLOCK)
                target[level, i, 0:BLOCK, cut] = top
                target[level, i, BLOCK : 2 * BLOCK, cut] = top
                target[level, i, 2 * BLOCK : 3 * BLOCK, cut] = rest

    def thrice(value, operator):
        top, rest = halves(value)
        return jnp.dot(
            jnp.concatenate([top, rest, top], 1), operator, preferred_element_type=jnp.float32
        )

    def eliminate(level, block_at):
        _, _, links, _, result = front_data[level]
        live_count = front_rows[0, level]
        values = []
        for i in range(RED):
            live = (lanes + i * BLOCK < live_count).astype(jnp.float32)
            value = live * thrice(live * block_at(i), front_solve[level, i])
            result[:, i * BLOCK : (i + 1) * BLOCK] = value
            values.append(value)
        pushed = []
        for i in range(RED):
            product = thrice(values[i], front_push[level, i])
            for k in range(LINKS):
                pushed.append((links[i, k], product[:, k * BLOCK : (k + 1) * BLOCK]))
        for j in range(SKELETONS[level]):
            update = jnp.zeros((2 * ROWS, BLOCK), jnp.float32)
            for link, product in pushed:
                update += jnp.where(link == j, 1.0, 0.0) * product
            updated[level, j] = block_at(RED + j) - update

    def join(level, half_at, to):
        half = SKELETONS[level] // 2
        copy = send(
            updated.at[level, pl.ds((1 - half_at) * half, half)],
            joined[level].at[pl.ds(half_at * half, half)],
            to,
        )
        for j in range(half):
            joined[level][half_at * half + j] = updated[level, half_at * half + j]
        return copy

    def ordered(level):
        order = front_data[level][3]
        return lambda k: joined[level][order[0, k]]

    prepare(0)
    first_load.wait()
    eliminate(0, lambda k: first_rows[:, k * BLOCK : (k + 1) * BLOCK])
    prepare(1)
    prepare(2)
    meet()
    joining = join(0, core, twin)
    factors = [send(factor_of[k], sibling.at[k], twin) for k in range(3)]
    joining.wait_recv()
    eliminate(1, ordered(0))
    joining = join(1, z_lo % 2, neighbour)
    joining.wait_recv()
    eliminate(2, ordered(1))
    for j in range(SKELETONS[2]):
        joined[2][j] = updated[2, j]
    last_block = ordered(2)
    for k in range(SKELETONS[2]):
        section[k // 2, :, k % 2 * BLOCK : (k % 2 + 1) * BLOCK] = last_block(k)

    mine_at = pl.multiple_of(core * HALF, HALF)
    other_at = pl.multiple_of(other * HALF, HALF)
    kept = pl.ds(pl.multiple_of(core * ROWS, ROWS), ROWS)
    given = pl.ds(pl.multiple_of(other * ROWS, ROWS), ROWS)
    swaps = [
        send(section.at[p, given, :], pieces.at[p, :, pl.ds(mine_at, HALF)], twin)
        for p in range(2)
    ]
    for p in range(2):
        pieces[p, :, pl.ds(mine_at, HALF)] = section[p, kept, :]

    def split(k):
        for source, at in ((own, mine_at), (sibling, other_at)):
            if source is own:
                loads[k].wait()
            else:
                factors[k].wait_recv()
            value = source[k]
            high[k, pl.ds(at, HALF), :], low[k, pl.ds(at, HALF), :] = halves(value)

    def multiply(step, k, transposed):
        top, rest = halves(gathered[step])
        both = jnp.concatenate([top, rest], 0)
        for half in range(2):
            cut = slice(half * HALF, (half + 1) * HALF)
            if transposed:
                right_high, right_low = high[k, cut, :], low[k, cut, :]
            else:
                right_high, right_low = high[k, :, cut], low[k, :, cut]
            dims = (((1,), (1 if transposed else 0,)), ((), ()))
            wide = lax.dot_general(both, right_high, dims, preferred_element_type=jnp.float32)
            thin = lax.dot_general(top, right_low, dims, preferred_element_type=jnp.float32)
            partial[step, :, cut] = wide[:TOTAL] + (wide[TOTAL:] + thin)

    def reduce_leaf(step, meanwhile):
        copies = []
        for n, (a, b) in enumerate(leaf_steps):
            group = lax.rem(x + a, SIDE) * SIDE + lax.rem(z_lo + b, SIDE)
            copies.append(
                send(partial.at[step, rows_of(group)], leaf_in.at[step, n], leaf_targets[n])
            )
        flush(len(pending) - len(copies))
        meanwhile()
        wait_all(copies)
        parts = [partial[step, rows_of(chip_row)]] + [leaf_in[step, n] for n in range(len(copies))]
        while len(parts) > 1:
            parts = [sum(parts[i : i + 2][1:], parts[i]) for i in range(0, len(parts), 2)]
        return parts[0]

    def gather_forward(step, piece):
        copies = turn(piece, moved.at[step - 1, rows_of(z_lo)], depth_forward)
        flush(len(pending) - SIDE)
        wait_all(copies)
        copies = turn(moved.at[step - 1], gathered.at[step, band_of(x)], plane_forward)
        flush(len(pending) - SIDE)
        wait_all(copies)

    def reduce_turned(at, pieces_at, slots, route, meanwhile):
        targets, itself, slot = route
        base = take(SIDE)
        for k in range(SIDE):
            send_unless_same(
                pieces_at(k), slots.at[at, slot], targets[k], itself[k], base + k, base + slot
            )
        flush(len(pending) - SIDE)
        meanwhile()
        for k in range(SIDE):
            pltpu.make_async_remote_copy(
                src_ref=slots.at[at, k],
                dst_ref=slots.at[at, k],
                send_sem=send_sem.at[base + k],
                recv_sem=recv_sem.at[base + k],
                device_id=twin,
                device_id_type=MESH,
            ).wait_recv()
        return (slots[at, 0] + slots[at, 1]) + (slots[at, 2] + slots[at, 3])

    def reduce_backward(step, meanwhile):
        at = step - 3
        first_sum[at] = reduce_turned(
            at,
            lambda k: partial.at[step, k * SIDE * ROWS : (k + 1) * SIDE * ROWS],
            first_in,
            plane_backward,
            meanwhile,
        )
        return reduce_turned(
            at,
            lambda k: first_sum.at[at, k * ROWS : (k + 1) * ROWS],
            second_in,
            depth_backward,
            nothing,
        )

    def gather_leaf(step, piece, meanwhile):
        copies = [send(piece, gathered.at[step, rows_of(chip_row)], to) for to in leaf_targets]
        gathered[step, rows_of(chip_row)] = piece[...]
        flush(len(pending) - len(copies))
        meanwhile()
        wait_all(copies)

    def give_result(source, panel):
        copy = send(source.at[:, pl.ds(other_at, HALF)], final_in.at[panel], twin)
        out[kept, panel * HALF : (panel + 1) * HALF] = source[:, pl.ds(mine_at, HALF)]
        return copy

    def take_result(copy, panel):
        copy.wait_recv()
        out[given, panel * HALF : (panel + 1) * HALF] = final_in[panel]

    def nothing():
        pass

    wait_all(swaps)
    copies = [
        send(pieces.at[0], gathered.at[0, rows_of(col)], around("z_hi", d)) for d in (2, 1, 3)
    ]
    n = take(1)
    sinking = send_unless_same(pieces.at[1], turned.at[0], sunk, same_depth, n, n)
    gathered[0, rows_of(col)] = pieces[0]
    split(0)
    wait_all(copies)
    band = gathered.at[0, band_of(y)]
    copies = [send(band, band, around("y", d)) for d in (2, 1, 3)]
    flush(len(pending) - len(copies))
    wait_all(copies)

    multiply(0, 0, False)
    solved[0] = reduce_leaf(0, lambda: split(1))
    gather_forward(1, solved.at[0])

    multiply(1, 1, False)
    turning = []

    def turn_on():
        split(2)
        sinking.wait_recv()
        n = take(1)
        turning.append(
            send_unless_same(turned.at[0], turned.at[1], flipped, same_plane, n, n)
        )

    total = reduce_leaf(1, turn_on)
    turning[0].wait_recv()
    solved[1] = turned[1] - total
    gather_forward(2, solved.at[1])

    multiply(2, 2, False)
    solved[2] = reduce_leaf(2, nothing)
    gather_leaf(3, solved.at[2], nothing)

    multiply(3, 2, True)
    solved[3] = reduce_backward(3, nothing)
    n = take(1)
    sinking_last = send_unless_same(solved.at[3], solved.at[4], sunk, same_depth, n, n)
    gather_leaf(4, solved.at[3], nothing)

    multiply(4, 1, True)
    handed = []

    def turn_last():
        sinking_last.wait_recv()
        n = take(1)
        handed.append(send_unless_same(solved.at[4], crossed, flipped, same_plane, n, n))

    def hand_last():
        handed[0].wait_recv()
        handed.append(give_result(crossed, 1))

    total = reduce_backward(4, turn_last)
    solved[5] = solved[0] - total
    gather_leaf(5, solved.at[5], hand_last)

    multiply(5, 0, True)
    copies = []
    for d in (2, 1, 3):
        to = lax.rem(y + d, SIDE)
        copies.append(
            send(partial.at[5, band_of(to)], first_in.at[2, d - 1], around("y", d))
        )
    flush(len(pending) - len(copies))
    wait_all(copies)
    total = partial[5, band_of(y)]
    first_sum[2] = total + first_in[2, 0] + (first_in[2, 1] + first_in[2, 2])
    copies = []
    for d in (2, 1, 3):
        to = lax.rem(z_hi + d, SIDE)
        copies.append(
            send(first_sum.at[2, rows_of(to)], second_in.at[2, d - 1], around("z_hi", d))
        )
    flush(len(pending) - len(copies))
    take_result(handed[1], 1)
    wait_all(copies)
    total = first_sum[2, rows_of(z_hi)]
    solved[6] = total + second_in[2, 0] + (second_in[2, 1] + second_in[2, 2])
    first = give_result(solved.at[6], 0)
    take_result(first, 0)
    flush(len(pending))


def hand_over(first, second, third, root, out_first, out_second, out_third, out_root):
    out_first[...] = first[...]
    out_second[...] = second[...]
    out_third[...] = third[...]
    for p in range(2):
        out_root[:, p, :] = root[:, p * HALF : (p + 1) * HALF]


def local(*operands):
    f32, bf16 = jnp.float32, jnp.bfloat16
    rhs_rows = operands[0].shape[0]
    vmem = pl.BlockSpec(memory_space=pltpu.VMEM)
    smem = pl.BlockSpec(memory_space=pltpu.SMEM)
    whole = pl.BlockSpec(memory_space=pltpu.HBM)
    outputs = pl.pallas_call(
        solve_kernel,
        out_shape=[jax.ShapeDtypeStruct((rhs_rows, SPAN), f32)] * 4,
        in_specs=[whole] + [whole, whole, smem, smem] * 3 + [smem, whole, whole],
        out_specs=[vmem] * 4,
        scratch_shapes=[
            pltpu.VMEM((2 * ROWS, GROUPS * BLOCK), f32),
            pltpu.VMEM((3, RED, BLOCK, BLOCK), f32),
            pltpu.VMEM((3, RED, LINKS, BLOCK, BLOCK), f32),
            pltpu.VMEM((3, RED, 3 * BLOCK, BLOCK), bf16),
            pltpu.VMEM((3, RED, 3 * BLOCK, LINKS * BLOCK), bf16),
            pltpu.VMEM((3, SKELETONS[0], 2 * ROWS, BLOCK), f32),
            pltpu.VMEM((SKELETONS[0], 2 * ROWS, BLOCK), f32),
            pltpu.VMEM((SKELETONS[1], 2 * ROWS, BLOCK), f32),
            pltpu.VMEM((SKELETONS[2], 2 * ROWS, BLOCK), f32),
            pltpu.VMEM((2, 2 * ROWS, HALF), f32),
            pltpu.VMEM((3, HALF, SPAN), f32),
            pltpu.VMEM((3, HALF, SPAN), f32),
            pltpu.VMEM((3, SPAN, SPAN), bf16),
            pltpu.VMEM((3, SPAN, SPAN), bf16),
            pltpu.VMEM((2, ROWS, SPAN), f32),
            pltpu.VMEM((2, ROWS, SPAN), f32),
            pltpu.VMEM((ROWS, SPAN), f32),
            pltpu.VMEM((2, SIDE * ROWS, SPAN), f32),
            pltpu.VMEM((STEPS, TOTAL, SPAN), f32),
            pltpu.VMEM((STEPS, TOTAL, SPAN), f32),
            pltpu.VMEM((3, GROUPS - 1, ROWS, SPAN), f32),
            pltpu.VMEM((3, SIDE, SIDE * ROWS, SPAN), f32),
            pltpu.VMEM((3, SIDE * ROWS, SPAN), f32),
            pltpu.VMEM((3, SIDE, ROWS, SPAN), f32),
            pltpu.VMEM((7, ROWS, SPAN), f32),
            pltpu.VMEM((2, ROWS, HALF), f32),
            pltpu.SemaphoreType.DMA((MESSAGES,)),
            pltpu.SemaphoreType.DMA((MESSAGES,)),
            pltpu.SemaphoreType.DMA((10,)),
        ],
        compiler_params=pltpu.CompilerParams(
            collective_id=0, has_side_effects=True, vmem_limit_bytes=63 << 20
        ),
        name="solve",
    )(*operands[:13], operands[13].T, *operands[14:])
    shapes = [jax.ShapeDtypeStruct((rhs_rows, SPAN), f32)] * 3
    return pl.pallas_call(
        hand_over,
        out_shape=[*shapes, jax.ShapeDtypeStruct((rhs_rows, 2, HALF), f32)],
        in_specs=[vmem] * 4,
        out_specs=[vmem] * 4,
        name="hand_over",
    )(*outputs)


def solution(mesh):
    in_specs = (
        P("col", "leaf"),
        P("leaf", None, None),
        P("leaf", None, None, None),
        P("leaf", None),
        P("leaf", None),
        P("leaf", None, None),
        P("leaf", None, None, None),
        P("leaf", None),
        P("leaf", None),
        P("leaf", None, None),
        P("leaf", None, None, None),
        P("leaf", None),
        P("leaf", None),
        P(None, "leaf"),
        P(None, "leaf", "col"),
        P("leaf", "col"),
    )
    out_specs = (P("col", "leaf"), P("col", "leaf"), P("col", "leaf"), P("col", None, "leaf"))
    return jax.shard_map(local, mesh=mesh, in_specs=in_specs, out_specs=out_specs, check_vma=False)
```

```python
import jax
import jax.numpy as jnp
from jax import lax
from jax.experimental import pallas as pl
from jax.experimental.pallas import tpu as pltpu
from jax.sharding import PartitionSpec as P

MESH = pl.DeviceIdType.MESH
SIDE = 4
ROWS = 8
GROUPS = SIDE * SIDE
TOTAL = GROUPS * ROWS
HALF = 256
SPAN = 512
BLOCK = 128
RED = 4
LINKS = 3
SKELETONS = (12, 8, 4)
STEPS = 6
MESSAGES = 240


def device(x, z_lo, core, y, z_hi):
    return (x * (2 * SIDE) + z_lo * 2 + core, y * SIDE + z_hi)


def rows_of(group):
    return pl.ds(pl.multiple_of(group * ROWS, ROWS), ROWS)


def band_of(member):
    return pl.ds(pl.multiple_of(member * SIDE * ROWS, SIDE * ROWS), SIDE * ROWS)


def solve_kernel(
    right_sides,
    inverse_first,
    coupling_first,
    links_first,
    order_first,
    inverse_second,
    coupling_second,
    links_second,
    order_second,
    inverse_third,
    coupling_third,
    links_third,
    order_third,
    front_rows,
    root_inverse,
    root_coupling,
    out_first,
    out_second,
    out_third,
    out,
    first_rows,
    front_inverse,
    front_coupling,
    front_solve,
    front_push,
    updated,
    joined_first,
    joined_second,
    joined_third,
    section,
    own,
    sibling,
    high,
    low,
    pieces,
    turned,
    crossed,
    moved,
    gathered,
    partial,
    leaf_in,
    first_in,
    first_sum,
    second_in,
    solved,
    final_in,
    send_sem,
    recv_sem,
    local_sem,
):
    leaf, col = lax.axis_index("leaf"), lax.axis_index("col")
    x, z_lo, core = leaf // (2 * SIDE), leaf // 2 % SIDE, leaf % 2
    y, z_hi = col // SIDE, col % SIDE
    chip_row = leaf // 2
    other = 1 - core
    same_plane = x == y
    same_depth = z_lo == z_hi

    def around(axis, step):
        at = {"x": x, "z_lo": z_lo, "y": y, "z_hi": z_hi}
        at[axis] = lax.rem(at[axis] + step, SIDE)
        return device(at["x"], at["z_lo"], core, at["y"], at["z_hi"])

    twin = device(x, z_lo, other, y, z_hi)
    neighbour = device(x, z_lo + 1 - 2 * (z_lo % 2), core, y, z_hi)
    sunk = device(x, z_hi, core, y, z_lo)
    flipped = device(y, z_lo, core, x, z_hi)
    leaf_steps = [(a, b) for a in (2, 1, 3, 0) for b in (3, 2, 1, 0) if a or b]
    leaf_targets = [
        device(lax.rem(x + a, SIDE), lax.rem(z_lo + b, SIDE), core, y, z_hi) for a, b in leaf_steps
    ]
    depth_forward = (
        [device(x, z_hi, core, y, k) for k in range(SIDE)],
        [jnp.logical_and(same_depth, z_hi == k) for k in range(SIDE)],
        z_lo,
    )
    depth_backward = (
        [device(x, k, core, y, z_lo) for k in range(SIDE)],
        [jnp.logical_and(same_depth, z_lo == k) for k in range(SIDE)],
        z_hi,
    )
    plane_forward = (
        [device(y, z_lo, core, k, z_hi) for k in range(SIDE)],
        [jnp.logical_and(same_plane, y == k) for k in range(SIDE)],
        x,
    )
    plane_backward = (
        [device(k, z_lo, core, x, z_hi) for k in range(SIDE)],
        [jnp.logical_and(same_plane, x == k) for k in range(SIDE)],
        y,
    )

    front_data = (
        (inverse_first, coupling_first, links_first, order_first, out_first),
        (inverse_second, coupling_second, links_second, order_second, out_second),
        (inverse_third, coupling_third, links_third, order_third, out_third),
    )
    first_load = pltpu.make_async_copy(right_sides, first_rows, local_sem.at[9])
    first_load.start()
    front_loads = []
    for level in range(3):
        pair = (
            pltpu.make_async_copy(
                front_data[level][0], front_inverse.at[level], local_sem.at[2 * level]
            ),
            pltpu.make_async_copy(
                front_data[level][1], front_coupling.at[level], local_sem.at[2 * level + 1]
            ),
        )
        for load in pair:
            load.start()
        front_loads.append(pair)
    factor_of = (root_inverse.at[0], root_coupling, root_inverse.at[1])
    loads = []
    for k in range(3):
        loads.append(pltpu.make_async_copy(factor_of[k], own.at[k], local_sem.at[6 + k]))
        loads[-1].start()

    barrier = pltpu.get_barrier_semaphore()

    def greet(to):
        pl.semaphore_signal(barrier, inc=1, device_id=to, device_id_type=MESH)

    for targets, itself, _ in (depth_forward, depth_backward, plane_forward, plane_backward):
        for k in range(SIDE):

            @pl.when(jnp.logical_not(itself[k]))
            def _():
                greet(targets[k])

    for axis in ("z_hi", "y"):
        for step in (2, 1, 3):
            greet(around(axis, step))
    for to in leaf_targets:
        greet(to)
    greet(twin)

    def meet():
        pl.semaphore_wait(
            barrier,
            1
            + (GROUPS - 1)
            + 2 * (SIDE - 1)
            + 4 * SIDE
            - 2 * same_plane.astype(jnp.int32)
            - 2 * same_depth.astype(jnp.int32),
        )

    used = [0]
    pending = []

    def take(count):
        used[0] += count
        return used[0] - count

    def send(source, target, to):
        n = take(1)
        copy = pltpu.make_async_remote_copy(
            src_ref=source,
            dst_ref=target,
            send_sem=send_sem.at[n],
            recv_sem=recv_sem.at[n],
            device_id=to,
            device_id_type=MESH,
        )
        copy.start()
        pending.append(copy.wait_send)
        return copy

    def send_unless_same(source, target, to, itself, sent, received):
        remote = pltpu.make_async_remote_copy(
            src_ref=source,
            dst_ref=target,
            send_sem=send_sem.at[sent],
            recv_sem=recv_sem.at[received],
            device_id=to,
            device_id_type=MESH,
        )

        @pl.when(jnp.logical_not(itself))
        def _():
            remote.start()

        @pl.when(itself)
        def _():
            pltpu.make_async_copy(source, target, recv_sem.at[received]).start()

        def finish():
            @pl.when(jnp.logical_not(itself))
            def _():
                remote.wait_send()

        pending.append(finish)
        return remote

    def flush(count):
        for finish in pending[:count]:
            finish()
        del pending[:count]

    def wait_all(copies):
        for copy in copies:
            copy.wait_recv()

    def turn(source, target, route):
        targets, itself, slot = route
        base = take(SIDE)
        for k in range(SIDE):
            send_unless_same(source, target, targets[k], itself[k], base + k, base + slot)
        return [
            pltpu.make_async_remote_copy(
                src_ref=source,
                dst_ref=target,
                send_sem=send_sem.at[base + k],
                recv_sem=recv_sem.at[base + k],
                device_id=twin,
                device_id_type=MESH,
            )
            for k in range(SIDE)
        ]

    def wait_slots(base, slots):
        for k in range(SIDE):
            pltpu.make_async_remote_copy(
                src_ref=slots.at[k],
                dst_ref=slots.at[k],
                send_sem=send_sem.at[base + k],
                recv_sem=recv_sem.at[base + k],
                device_id=twin,
                device_id_type=MESH,
            ).wait_recv()

    def sum_slots(slots, *at):
        return (slots[*at, 0] + slots[*at, 1]) + (slots[*at, 2] + slots[*at, 3])

    joined = (joined_first, joined_second, joined_third)
    lanes = lax.broadcasted_iota(jnp.int32, (2 * ROWS, BLOCK), 1)

    def halves(value):
        top = value.astype(jnp.bfloat16)
        return top, (value - top.astype(jnp.float32)).astype(jnp.bfloat16)

    def prepare(level):
        for load in front_loads[level]:
            load.wait()
        for i in range(RED):
            parts = [(front_solve, 0, front_inverse[level, i])]
            parts += [(front_push, k, front_coupling[level, i, k]) for k in range(LINKS)]
            for target, k, value in parts:
                top, rest = halves(value)
                cut = slice(k * BLOCK, (k + 1) * BLOCK)
                target[level, i, 0:BLOCK, cut] = top
                target[level, i, BLOCK : 2 * BLOCK, cut] = top
                target[level, i, 2 * BLOCK : 3 * BLOCK, cut] = rest

    def thrice(value, operator):
        top, rest = halves(value)
        return jnp.dot(
            jnp.concatenate([top, rest, top], 1), operator, preferred_element_type=jnp.float32
        )

    def eliminate(level, block_at):
        _, _, links, _, result = front_data[level]
        live_count = front_rows[0, level]
        values = []
        for i in range(RED):
            live = (lanes + i * BLOCK < live_count).astype(jnp.float32)
            value = live * thrice(live * block_at(i), front_solve[level, i])
            result[:, i * BLOCK : (i + 1) * BLOCK] = value
            values.append(value)
        pushed = []
        for i in range(RED):
            product = thrice(values[i], front_push[level, i])
            for k in range(LINKS):
                pushed.append((links[i, k], product[:, k * BLOCK : (k + 1) * BLOCK]))
        for j in range(SKELETONS[level]):
            update = jnp.zeros((2 * ROWS, BLOCK), jnp.float32)
            for link, product in pushed:
                update += jnp.where(link == j, 1.0, 0.0) * product
            updated[level, j] = block_at(RED + j) - update

    def join(level, half_at, to):
        half = SKELETONS[level] // 2
        copy = send(
            updated.at[level, pl.ds((1 - half_at) * half, half)],
            joined[level].at[pl.ds(half_at * half, half)],
            to,
        )
        for j in range(half):
            joined[level][half_at * half + j] = updated[level, half_at * half + j]
        return copy

    def ordered(level):
        order = front_data[level][3]
        return lambda k: joined[level][order[0, k]]

    prepare(0)
    first_load.wait()
    eliminate(0, lambda k: first_rows[:, k * BLOCK : (k + 1) * BLOCK])
    prepare(1)
    prepare(2)
    meet()
    joining = join(0, core, twin)
    factors = [send(factor_of[k], sibling.at[k], twin) for k in range(3)]
    joining.wait_recv()
    eliminate(1, ordered(0))
    joining = join(1, z_lo % 2, neighbour)
    joining.wait_recv()
    eliminate(2, ordered(1))
    for j in range(SKELETONS[2]):
        joined[2][j] = updated[2, j]
    last_block = ordered(2)
    for k in range(SKELETONS[2]):
        section[k // 2, :, k % 2 * BLOCK : (k % 2 + 1) * BLOCK] = last_block(k)

    mine_at = pl.multiple_of(core * HALF, HALF)
    other_at = pl.multiple_of(other * HALF, HALF)
    kept = pl.ds(pl.multiple_of(core * ROWS, ROWS), ROWS)
    given = pl.ds(pl.multiple_of(other * ROWS, ROWS), ROWS)
    swaps = [
        send(section.at[p, given, :], pieces.at[p, :, pl.ds(mine_at, HALF)], twin)
        for p in range(2)
    ]
    for p in range(2):
        pieces[p, :, pl.ds(mine_at, HALF)] = section[p, kept, :]

    def split(k):
        for source, at in ((own, mine_at), (sibling, other_at)):
            if source is own:
                loads[k].wait()
            else:
                factors[k].wait_recv()
            value = source[k]
            high[k, pl.ds(at, HALF), :], low[k, pl.ds(at, HALF), :] = halves(value)

    def multiply(step, k, transposed):
        top, rest = halves(gathered[step])
        both = jnp.concatenate([top, rest], 0)
        for half in range(2):
            cut = slice(half * HALF, (half + 1) * HALF)
            if transposed:
                right_high, right_low = high[k, cut, :], low[k, cut, :]
            else:
                right_high, right_low = high[k, :, cut], low[k, :, cut]
            dims = (((1,), (1 if transposed else 0,)), ((), ()))
            wide = lax.dot_general(both, right_high, dims, preferred_element_type=jnp.float32)
            thin = lax.dot_general(top, right_low, dims, preferred_element_type=jnp.float32)
            partial[step, :, cut] = wide[:TOTAL] + (wide[TOTAL:] + thin)

    def reduce_leaf(step, meanwhile):
        copies = []
        for n, (a, b) in enumerate(leaf_steps):
            group = lax.rem(x + a, SIDE) * SIDE + lax.rem(z_lo + b, SIDE)
            copies.append(
                send(partial.at[step, rows_of(group)], leaf_in.at[step, n], leaf_targets[n])
            )
        flush(len(pending) - len(copies))
        meanwhile()
        wait_all(copies)
        parts = [partial[step, rows_of(chip_row)]] + [leaf_in[step, n] for n in range(len(copies))]
        while len(parts) > 1:
            parts = [sum(parts[i : i + 2][1:], parts[i]) for i in range(0, len(parts), 2)]
        return parts[0]

    def gather_forward(step, piece):
        copies = turn(piece, moved.at[step - 1, rows_of(z_lo)], depth_forward)
        flush(len(pending) - SIDE)
        onward = []
        for k in range(SIDE):
            copies[k].wait_recv()
            onward += turn(
                moved.at[step - 1, k * ROWS : (k + 1) * ROWS],
                gathered.at[step, rows_of(x * SIDE + k)],
                plane_forward,
            )
        flush(len(pending) - len(onward))
        wait_all(onward)

    def reduce_backward(step, meanwhile):
        at = step - 3
        arriving = []
        for k in range(SIDE):
            targets, itself, slot = plane_backward
            base = take(SIDE)
            for band in range(SIDE):
                row = (band * SIDE + k) * ROWS
                send_unless_same(
                    partial.at[step, row : row + ROWS],
                    first_in.at[at, k, slot],
                    targets[band],
                    itself[band],
                    base + band,
                    base + slot,
                )
            arriving.append(base)
        flush(len(pending) - GROUPS)
        meanwhile()
        targets, itself, slot = depth_backward
        last = take(SIDE)
        for k in range(SIDE):
            wait_slots(arriving[k], first_in.at[at, k])
            first_sum[at, k * ROWS : (k + 1) * ROWS] = sum_slots(first_in, at, k)
            send_unless_same(
                first_sum.at[at, k * ROWS : (k + 1) * ROWS],
                second_in.at[at, slot],
                targets[k],
                itself[k],
                last + k,
                last + slot,
            )
        flush(len(pending) - SIDE)
        wait_slots(last, second_in.at[at])
        return sum_slots(second_in, at)

    def gather_leaf(step, piece, meanwhile):
        copies = [send(piece, gathered.at[step, rows_of(chip_row)], to) for to in leaf_targets]
        gathered[step, rows_of(chip_row)] = piece[...]
        flush(len(pending) - len(copies))
        meanwhile()
        wait_all(copies)

    def give_result(source, panel):
        copy = send(source.at[:, pl.ds(other_at, HALF)], final_in.at[panel], twin)
        out[kept, panel * HALF : (panel + 1) * HALF] = source[:, pl.ds(mine_at, HALF)]
        return copy

    def take_result(copy, panel):
        copy.wait_recv()
        out[given, panel * HALF : (panel + 1) * HALF] = final_in[panel]

    def nothing():
        pass

    wait_all(swaps)
    copies = [
        send(pieces.at[0], gathered.at[0, rows_of(col)], around("z_hi", d)) for d in (2, 1, 3)
    ]
    n = take(1)
    sinking = send_unless_same(pieces.at[1], turned.at[0], sunk, same_depth, n, n)
    gathered[0, rows_of(col)] = pieces[0]
    onward = [
        send(pieces.at[0], gathered.at[0, rows_of(col)], around("y", d)) for d in (2, 1, 3)
    ]
    split(0)
    for n, step in ((1, 1), (2, 3), (0, 2)):
        copies[n].wait_recv()
        band = gathered.at[0, rows_of(y * SIDE + lax.rem(z_hi + SIDE - step, SIDE))]
        onward += [send(band, band, around("y", d)) for d in (2, 1, 3)]
    flush(len(pending) - len(onward))
    wait_all(onward)

    multiply(0, 0, False)
    solved[0] = reduce_leaf(0, lambda: split(1))
    gather_forward(1, solved.at[0])

    multiply(1, 1, False)
    turning = []

    def turn_on():
        split(2)
        sinking.wait_recv()
        n = take(1)
        turning.append(
            send_unless_same(turned.at[0], turned.at[1], flipped, same_plane, n, n)
        )

    total = reduce_leaf(1, turn_on)
    turning[0].wait_recv()
    solved[1] = turned[1] - total
    gather_forward(2, solved.at[1])

    multiply(2, 2, False)
    solved[2] = reduce_leaf(2, nothing)
    gather_leaf(3, solved.at[2], nothing)

    multiply(3, 2, True)
    solved[3] = reduce_backward(3, nothing)
    n = take(1)
    sinking_last = send_unless_same(solved.at[3], solved.at[4], sunk, same_depth, n, n)
    gather_leaf(4, solved.at[3], nothing)

    multiply(4, 1, True)
    handed = []

    def turn_last():
        sinking_last.wait_recv()
        n = take(1)
        handed.append(send_unless_same(solved.at[4], crossed, flipped, same_plane, n, n))

    def hand_last():
        handed[0].wait_recv()
        handed.append(give_result(crossed, 1))

    total = reduce_backward(4, turn_last)
    solved[5] = solved[0] - total
    gather_leaf(5, solved.at[5], hand_last)

    multiply(5, 0, True)
    order = (2, 1, 3, 0)
    arriving = []
    for n, d in enumerate(order):
        group = lax.rem(z_hi + d, SIDE)
        arriving.append(
            [
                send(
                    partial.at[5, rows_of(lax.rem(y + e, SIDE) * SIDE + group)],
                    first_in.at[2, n, e - 1],
                    around("y", e),
                )
                for e in (2, 1, 3)
            ]
        )
    flush(len(pending) - 4 * (SIDE - 1))
    copies = []
    for n, d in enumerate(order):
        group = lax.rem(z_hi + d, SIDE)
        wait_all(arriving[n])
        total = partial[5, rows_of(y * SIDE + group)]
        first_sum[2, n * ROWS : (n + 1) * ROWS] = (
            total + first_in[2, n, 0] + (first_in[2, n, 1] + first_in[2, n, 2])
        )
        if d:
            copies.append(
                send(
                    first_sum.at[2, n * ROWS : (n + 1) * ROWS],
                    second_in.at[2, d - 1],
                    around("z_hi", d),
                )
            )
    flush(len(pending) - len(copies))
    take_result(handed[1], 1)
    wait_all(copies)
    total = first_sum[2, 3 * ROWS : 4 * ROWS]
    solved[6] = total + second_in[2, 0] + (second_in[2, 1] + second_in[2, 2])
    first = give_result(solved.at[6], 0)
    take_result(first, 0)
    flush(len(pending))


def hand_over(first, second, third, root, out_first, out_second, out_third, out_root):
    out_first[...] = first[...]
    out_second[...] = second[...]
    out_third[...] = third[...]
    for p in range(2):
        out_root[:, p, :] = root[:, p * HALF : (p + 1) * HALF]


def local(*operands):
    f32, bf16 = jnp.float32, jnp.bfloat16
    rhs_rows = operands[0].shape[0]
    vmem = pl.BlockSpec(memory_space=pltpu.VMEM)
    smem = pl.BlockSpec(memory_space=pltpu.SMEM)
    whole = pl.BlockSpec(memory_space=pltpu.HBM)
    outputs = pl.pallas_call(
        solve_kernel,
        out_shape=[jax.ShapeDtypeStruct((rhs_rows, SPAN), f32)] * 4,
        in_specs=[whole] + [whole, whole, smem, smem] * 3 + [smem, whole, whole],
        out_specs=[vmem] * 4,
        scratch_shapes=[
            pltpu.VMEM((2 * ROWS, GROUPS * BLOCK), f32),
            pltpu.VMEM((3, RED, BLOCK, BLOCK), f32),
            pltpu.VMEM((3, RED, LINKS, BLOCK, BLOCK), f32),
            pltpu.VMEM((3, RED, 3 * BLOCK, BLOCK), bf16),
            pltpu.VMEM((3, RED, 3 * BLOCK, LINKS * BLOCK), bf16),
            pltpu.VMEM((3, SKELETONS[0], 2 * ROWS, BLOCK), f32),
            pltpu.VMEM((SKELETONS[0], 2 * ROWS, BLOCK), f32),
            pltpu.VMEM((SKELETONS[1], 2 * ROWS, BLOCK), f32),
            pltpu.VMEM((SKELETONS[2], 2 * ROWS, BLOCK), f32),
            pltpu.VMEM((2, 2 * ROWS, HALF), f32),
            pltpu.VMEM((3, HALF, SPAN), f32),
            pltpu.VMEM((3, HALF, SPAN), f32),
            pltpu.VMEM((3, SPAN, SPAN), bf16),
            pltpu.VMEM((3, SPAN, SPAN), bf16),
            pltpu.VMEM((2, ROWS, SPAN), f32),
            pltpu.VMEM((2, ROWS, SPAN), f32),
            pltpu.VMEM((ROWS, SPAN), f32),
            pltpu.VMEM((2, SIDE * ROWS, SPAN), f32),
            pltpu.VMEM((STEPS, TOTAL, SPAN), f32),
            pltpu.VMEM((STEPS, TOTAL, SPAN), f32),
            pltpu.VMEM((3, GROUPS - 1, ROWS, SPAN), f32),
            pltpu.VMEM((3, SIDE, SIDE, ROWS, SPAN), f32),
            pltpu.VMEM((3, SIDE * ROWS, SPAN), f32),
            pltpu.VMEM((3, SIDE, ROWS, SPAN), f32),
            pltpu.VMEM((7, ROWS, SPAN), f32),
            pltpu.VMEM((2, ROWS, HALF), f32),
            pltpu.SemaphoreType.DMA((MESSAGES,)),
            pltpu.SemaphoreType.DMA((MESSAGES,)),
            pltpu.SemaphoreType.DMA((10,)),
        ],
        compiler_params=pltpu.CompilerParams(
            collective_id=0, has_side_effects=True, vmem_limit_bytes=63 << 20
        ),
        name="solve",
    )(*operands[:13], operands[13].T, *operands[14:])
    shapes = [jax.ShapeDtypeStruct((rhs_rows, SPAN), f32)] * 3
    return pl.pallas_call(
        hand_over,
        out_shape=[*shapes, jax.ShapeDtypeStruct((rhs_rows, 2, HALF), f32)],
        in_specs=[vmem] * 4,
        out_specs=[vmem] * 4,
        name="hand_over",
    )(*outputs)


def solution(mesh):
    in_specs = (
        P("col", "leaf"),
        P("leaf", None, None),
        P("leaf", None, None, None),
        P("leaf", None),
        P("leaf", None),
        P("leaf", None, None),
        P("leaf", None, None, None),
        P("leaf", None),
        P("leaf", None),
        P("leaf", None, None),
        P("leaf", None, None, None),
        P("leaf", None),
        P("leaf", None),
        P(None, "leaf"),
        P(None, "leaf", "col"),
        P("leaf", "col"),
    )
    out_specs = (P("col", "leaf"), P("col", "leaf"), P("col", "leaf"), P("col", None, "leaf"))
    return jax.shard_map(local, mesh=mesh, in_specs=in_specs, out_specs=out_specs, check_vma=False)
```

```python
import jax
import jax.numpy as jnp
from jax import lax
from jax.experimental import pallas as pl
from jax.experimental.pallas import tpu as pltpu
from jax.sharding import PartitionSpec as P

MESH = pl.DeviceIdType.MESH
SIDE = 4
ROWS = 8
GROUPS = SIDE * SIDE
TOTAL = GROUPS * ROWS
HALF = 256
SPAN = 512
BLOCK = 128
RED = 4
LINKS = 3
SKELETONS = (12, 8, 4)
STEPS = 6
ORDER = (2, 1, 3, 0)
MESSAGES = 240


def device(x, z_lo, core, y, z_hi):
    return (x * (2 * SIDE) + z_lo * 2 + core, y * SIDE + z_hi)


def rows_of(group):
    return pl.ds(pl.multiple_of(group * ROWS, ROWS), ROWS)


def band_of(member):
    return pl.ds(pl.multiple_of(member * SIDE * ROWS, SIDE * ROWS), SIDE * ROWS)


def solve_kernel(
    right_sides,
    inverse_first,
    coupling_first,
    links_first,
    order_first,
    inverse_second,
    coupling_second,
    links_second,
    order_second,
    inverse_third,
    coupling_third,
    links_third,
    order_third,
    front_rows,
    root_inverse,
    root_coupling,
    out_first,
    out_second,
    out_third,
    out,
    first_rows,
    front_inverse,
    front_coupling,
    front_solve,
    front_push,
    updated,
    joined_first,
    joined_second,
    joined_third,
    section,
    own,
    sibling,
    high,
    low,
    pieces,
    turned,
    crossed,
    moved,
    gathered,
    partial,
    leaf_in,
    first_in,
    first_sum,
    second_in,
    solved,
    final_in,
    send_sem,
    recv_sem,
    local_sem,
):
    leaf, col = lax.axis_index("leaf"), lax.axis_index("col")
    x, z_lo, core = leaf // (2 * SIDE), leaf // 2 % SIDE, leaf % 2
    y, z_hi = col // SIDE, col % SIDE
    chip_row = leaf // 2
    other = 1 - core
    same_plane = x == y
    same_depth = z_lo == z_hi

    def around(axis, step):
        at = {"x": x, "z_lo": z_lo, "y": y, "z_hi": z_hi}
        at[axis] = lax.rem(at[axis] + step, SIDE)
        return device(at["x"], at["z_lo"], core, at["y"], at["z_hi"])

    twin = device(x, z_lo, other, y, z_hi)
    neighbour = device(x, z_lo + 1 - 2 * (z_lo % 2), core, y, z_hi)
    sunk = device(x, z_hi, core, y, z_lo)
    flipped = device(y, z_lo, core, x, z_hi)
    leaf_steps = [(a, b) for a in (2, 1, 3, 0) for b in (3, 2, 1, 0) if a or b]
    leaf_targets = [
        device(lax.rem(x + a, SIDE), lax.rem(z_lo + b, SIDE), core, y, z_hi) for a, b in leaf_steps
    ]
    depth_forward = (
        [device(x, z_hi, core, y, lax.rem(z_hi + d, SIDE)) for d in ORDER],
        same_depth,
        z_lo,
    )
    depth_backward = (
        [device(x, lax.rem(z_lo + d, SIDE), core, y, z_lo) for d in ORDER],
        same_depth,
        z_hi,
    )
    plane_forward = (
        [device(y, z_lo, core, lax.rem(y + d, SIDE), z_hi) for d in ORDER],
        same_plane,
        x,
    )
    plane_backward = (
        [device(lax.rem(x + d, SIDE), z_lo, core, x, z_hi) for d in ORDER],
        same_plane,
        y,
    )

    front_data = (
        (inverse_first, coupling_first, links_first, order_first, out_first),
        (inverse_second, coupling_second, links_second, order_second, out_second),
        (inverse_third, coupling_third, links_third, order_third, out_third),
    )
    first_load = pltpu.make_async_copy(right_sides, first_rows, local_sem.at[9])
    first_load.start()
    front_loads = []
    for level in range(3):
        pair = (
            pltpu.make_async_copy(
                front_data[level][0], front_inverse.at[level], local_sem.at[2 * level]
            ),
            pltpu.make_async_copy(
                front_data[level][1], front_coupling.at[level], local_sem.at[2 * level + 1]
            ),
        )
        for load in pair:
            load.start()
        front_loads.append(pair)
    factor_of = (root_inverse.at[0], root_coupling, root_inverse.at[1])
    loads = []
    for k in range(3):
        loads.append(pltpu.make_async_copy(factor_of[k], own.at[k], local_sem.at[6 + k]))
        loads[-1].start()

    barrier = pltpu.get_barrier_semaphore()

    def greet(to):
        pl.semaphore_signal(barrier, inc=1, device_id=to, device_id_type=MESH)

    for targets, itself, _ in (depth_forward, depth_backward, plane_forward, plane_backward):
        for to in targets[:-1]:
            greet(to)

        @pl.when(jnp.logical_not(itself))
        def _():
            greet(targets[-1])

    for axis in ("z_hi", "y"):
        for step in (2, 1, 3):
            greet(around(axis, step))
    for to in leaf_targets:
        greet(to)
    greet(twin)

    def meet():
        pl.semaphore_wait(
            barrier,
            1
            + (GROUPS - 1)
            + 2 * (SIDE - 1)
            + 4 * SIDE
            - 2 * same_plane.astype(jnp.int32)
            - 2 * same_depth.astype(jnp.int32),
        )

    used = [0]
    pending = []

    def take(count):
        used[0] += count
        return used[0] - count

    def send(source, target, to):
        n = take(1)
        copy = pltpu.make_async_remote_copy(
            src_ref=source,
            dst_ref=target,
            send_sem=send_sem.at[n],
            recv_sem=recv_sem.at[n],
            device_id=to,
            device_id_type=MESH,
        )
        copy.start()
        pending.append(copy.wait_send)
        return copy

    def send_unless_same(source, target, to, itself, sent, received):
        remote = pltpu.make_async_remote_copy(
            src_ref=source,
            dst_ref=target,
            send_sem=send_sem.at[sent],
            recv_sem=recv_sem.at[received],
            device_id=to,
            device_id_type=MESH,
        )

        if itself is None:
            remote.start()
            pending.append(remote.wait_send)
            return remote

        @pl.when(jnp.logical_not(itself))
        def _():
            remote.start()

        @pl.when(itself)
        def _():
            pltpu.make_async_copy(source, target, recv_sem.at[received]).start()

        def finish():
            @pl.when(jnp.logical_not(itself))
            def _():
                remote.wait_send()

        pending.append(finish)
        return remote

    def flush(count):
        for finish in pending[:count]:
            finish()
        del pending[:count]

    def wait_all(copies):
        for copy in copies:
            copy.wait_recv()

    def turn(source, target, route):
        targets, itself, slot = route
        base = take(SIDE)
        for n, d in enumerate(ORDER):
            send_unless_same(
                source, target, targets[n], None if d else itself, base + n, base + slot
            )
        return [
            pltpu.make_async_remote_copy(
                src_ref=source,
                dst_ref=target,
                send_sem=send_sem.at[base + k],
                recv_sem=recv_sem.at[base + k],
                device_id=twin,
                device_id_type=MESH,
            )
            for k in range(SIDE)
        ]

    def wait_slots(base, slots):
        for k in range(SIDE):
            pltpu.make_async_remote_copy(
                src_ref=slots.at[k],
                dst_ref=slots.at[k],
                send_sem=send_sem.at[base + k],
                recv_sem=recv_sem.at[base + k],
                device_id=twin,
                device_id_type=MESH,
            ).wait_recv()

    def sum_slots(slots, *at):
        return (slots[*at, 0] + slots[*at, 1]) + (slots[*at, 2] + slots[*at, 3])

    joined = (joined_first, joined_second, joined_third)
    lanes = lax.broadcasted_iota(jnp.int32, (2 * ROWS, BLOCK), 1)

    def halves(value):
        top = value.astype(jnp.bfloat16)
        return top, (value - top.astype(jnp.float32)).astype(jnp.bfloat16)

    def prepare(level):
        for load in front_loads[level]:
            load.wait()
        for i in range(RED):
            parts = [(front_solve, 0, front_inverse[level, i])]
            parts += [(front_push, k, front_coupling[level, i, k]) for k in range(LINKS)]
            for target, k, value in parts:
                top, rest = halves(value)
                cut = slice(k * BLOCK, (k + 1) * BLOCK)
                target[level, i, 0:BLOCK, cut] = top
                target[level, i, BLOCK : 2 * BLOCK, cut] = top
                target[level, i, 2 * BLOCK : 3 * BLOCK, cut] = rest

    def thrice(value, operator):
        top, rest = halves(value)
        return jnp.dot(
            jnp.concatenate([top, rest, top], 1), operator, preferred_element_type=jnp.float32
        )

    def eliminate(level, block_at):
        _, _, links, _, result = front_data[level]
        live_count = front_rows[0, level]
        values = []
        for i in range(RED):
            live = (lanes + i * BLOCK < live_count).astype(jnp.float32)
            value = live * thrice(live * block_at(i), front_solve[level, i])
            result[:, i * BLOCK : (i + 1) * BLOCK] = value
            values.append(value)
        pushed = []
        for i in range(RED):
            product = thrice(values[i], front_push[level, i])
            for k in range(LINKS):
                pushed.append((links[i, k], product[:, k * BLOCK : (k + 1) * BLOCK]))
        for j in range(SKELETONS[level]):
            update = jnp.zeros((2 * ROWS, BLOCK), jnp.float32)
            for link, product in pushed:
                update += jnp.where(link == j, 1.0, 0.0) * product
            updated[level, j] = block_at(RED + j) - update

    def join(level, half_at, to):
        half = SKELETONS[level] // 2
        copy = send(
            updated.at[level, pl.ds((1 - half_at) * half, half)],
            joined[level].at[pl.ds(half_at * half, half)],
            to,
        )
        for j in range(half):
            joined[level][half_at * half + j] = updated[level, half_at * half + j]
        return copy

    def ordered(level):
        order = front_data[level][3]
        return lambda k: joined[level][order[0, k]]

    prepare(0)
    first_load.wait()
    eliminate(0, lambda k: first_rows[:, k * BLOCK : (k + 1) * BLOCK])
    prepare(1)
    prepare(2)
    meet()
    joining = join(0, core, twin)
    factors = [send(factor_of[k], sibling.at[k], twin) for k in range(3)]
    joining.wait_recv()
    eliminate(1, ordered(0))
    joining = join(1, z_lo % 2, neighbour)
    joining.wait_recv()
    eliminate(2, ordered(1))
    for j in range(SKELETONS[2]):
        joined[2][j] = updated[2, j]
    last_block = ordered(2)
    for k in range(SKELETONS[2]):
        section[k // 2, :, k % 2 * BLOCK : (k % 2 + 1) * BLOCK] = last_block(k)

    mine_at = pl.multiple_of(core * HALF, HALF)
    other_at = pl.multiple_of(other * HALF, HALF)
    kept = pl.ds(pl.multiple_of(core * ROWS, ROWS), ROWS)
    given = pl.ds(pl.multiple_of(other * ROWS, ROWS), ROWS)
    swaps = [
        send(section.at[p, given, :], pieces.at[p, :, pl.ds(mine_at, HALF)], twin)
        for p in range(2)
    ]
    for p in range(2):
        pieces[p, :, pl.ds(mine_at, HALF)] = section[p, kept, :]

    def split(k):
        for source, at in ((own, mine_at), (sibling, other_at)):
            if source is own:
                loads[k].wait()
            else:
                factors[k].wait_recv()
            value = source[k]
            high[k, pl.ds(at, HALF), :], low[k, pl.ds(at, HALF), :] = halves(value)

    def multiply(step, k, transposed):
        top, rest = halves(gathered[step])
        both = jnp.concatenate([top, rest], 0)
        for half in range(2):
            cut = slice(half * HALF, (half + 1) * HALF)
            if transposed:
                right_high, right_low = high[k, cut, :], low[k, cut, :]
            else:
                right_high, right_low = high[k, :, cut], low[k, :, cut]
            dims = (((1,), (1 if transposed else 0,)), ((), ()))
            wide = lax.dot_general(both, right_high, dims, preferred_element_type=jnp.float32)
            thin = lax.dot_general(top, right_low, dims, preferred_element_type=jnp.float32)
            partial[step, :, cut] = wide[:TOTAL] + (wide[TOTAL:] + thin)

    def reduce_leaf(step, meanwhile):
        copies = []
        for n, (a, b) in enumerate(leaf_steps):
            group = lax.rem(x + a, SIDE) * SIDE + lax.rem(z_lo + b, SIDE)
            copies.append(
                send(partial.at[step, rows_of(group)], leaf_in.at[step, n], leaf_targets[n])
            )
        flush(len(pending) - len(copies))
        meanwhile()
        wait_all(copies)
        parts = [partial[step, rows_of(chip_row)]] + [leaf_in[step, n] for n in range(len(copies))]
        while len(parts) > 1:
            parts = [sum(parts[i : i + 2][1:], parts[i]) for i in range(0, len(parts), 2)]
        return parts[0]

    def gather_forward(step, piece):
        copies = turn(piece, moved.at[step - 1, rows_of(z_lo)], depth_forward)
        flush(len(pending) - SIDE)
        onward = []
        for k in range(SIDE):
            copies[k].wait_recv()
            onward += turn(
                moved.at[step - 1, k * ROWS : (k + 1) * ROWS],
                gathered.at[step, rows_of(x * SIDE + k)],
                plane_forward,
            )
        flush(len(pending) - len(onward))
        wait_all(onward)

    def reduce_backward(step, meanwhile):
        at = step - 3
        arriving = []
        for i, shift in enumerate(ORDER):
            targets, itself, slot = plane_backward
            base = take(SIDE)
            for n, d in enumerate(ORDER):
                group = lax.rem(x + d, SIDE) * SIDE + lax.rem(z_lo + shift, SIDE)
                send_unless_same(
                    partial.at[step, rows_of(group)],
                    first_in.at[at, i, slot],
                    targets[n],
                    None if d else itself,
                    base + n,
                    base + slot,
                )
            arriving.append(base)
        flush(len(pending) - GROUPS)
        meanwhile()
        targets, itself, slot = depth_backward
        last = take(SIDE)
        for k in range(SIDE):
            wait_slots(arriving[k], first_in.at[at, k])
            first_sum[at, k * ROWS : (k + 1) * ROWS] = sum_slots(first_in, at, k)
            send_unless_same(
                first_sum.at[at, k * ROWS : (k + 1) * ROWS],
                second_in.at[at, slot],
                targets[k],
                None if ORDER[k] else itself,
                last + k,
                last + slot,
            )
        flush(len(pending) - SIDE)
        wait_slots(last, second_in.at[at])
        return sum_slots(second_in, at)

    def gather_leaf(step, piece, meanwhile):
        copies = [send(piece, gathered.at[step, rows_of(chip_row)], to) for to in leaf_targets]
        gathered[step, rows_of(chip_row)] = piece[...]
        flush(len(pending) - len(copies))
        meanwhile()
        wait_all(copies)

    def give_result(source, panel):
        copy = send(source.at[:, pl.ds(other_at, HALF)], final_in.at[panel], twin)
        out[kept, panel * HALF : (panel + 1) * HALF] = source[:, pl.ds(mine_at, HALF)]
        return copy

    def take_result(copy, panel):
        copy.wait_recv()
        out[given, panel * HALF : (panel + 1) * HALF] = final_in[panel]

    def nothing():
        pass

    wait_all(swaps)
    copies = [
        send(pieces.at[0], gathered.at[0, rows_of(col)], around("z_hi", d)) for d in (2, 1, 3)
    ]
    n = take(1)
    sinking = send_unless_same(pieces.at[1], turned.at[0], sunk, same_depth, n, n)
    gathered[0, rows_of(col)] = pieces[0]
    onward = [
        send(pieces.at[0], gathered.at[0, rows_of(col)], around("y", d)) for d in (2, 1, 3)
    ]
    split(0)
    for n, step in ((1, 1), (2, 3), (0, 2)):
        copies[n].wait_recv()
        band = gathered.at[0, rows_of(y * SIDE + lax.rem(z_hi + SIDE - step, SIDE))]
        onward += [send(band, band, around("y", d)) for d in (2, 1, 3)]
    flush(len(pending) - len(onward))
    wait_all(onward)

    multiply(0, 0, False)
    solved[0] = reduce_leaf(0, lambda: split(1))
    gather_forward(1, solved.at[0])

    multiply(1, 1, False)
    turning = []

    def turn_on():
        split(2)
        sinking.wait_recv()
        n = take(1)
        turning.append(
            send_unless_same(turned.at[0], turned.at[1], flipped, same_plane, n, n)
        )

    total = reduce_leaf(1, turn_on)
    turning[0].wait_recv()
    solved[1] = turned[1] - total
    gather_forward(2, solved.at[1])

    multiply(2, 2, False)
    solved[2] = reduce_leaf(2, nothing)
    gather_leaf(3, solved.at[2], nothing)

    multiply(3, 2, True)
    solved[3] = reduce_backward(3, nothing)
    n = take(1)
    sinking_last = send_unless_same(solved.at[3], solved.at[4], sunk, same_depth, n, n)
    gather_leaf(4, solved.at[3], nothing)

    multiply(4, 1, True)
    handed = []

    def turn_last():
        sinking_last.wait_recv()
        n = take(1)
        handed.append(send_unless_same(solved.at[4], crossed, flipped, same_plane, n, n))

    def hand_last():
        handed[0].wait_recv()
        handed.append(give_result(crossed, 1))

    total = reduce_backward(4, turn_last)
    solved[5] = solved[0] - total
    gather_leaf(5, solved.at[5], hand_last)

    multiply(5, 0, True)
    order = (2, 1, 3, 0)
    arriving = []
    for n, d in enumerate(order):
        group = lax.rem(z_hi + d, SIDE)
        arriving.append(
            [
                send(
                    partial.at[5, rows_of(lax.rem(y + e, SIDE) * SIDE + group)],
                    first_in.at[2, n, e - 1],
                    around("y", e),
                )
                for e in (2, 1, 3)
            ]
        )
    flush(len(pending) - 4 * (SIDE - 1))
    copies = []
    for n, d in enumerate(order):
        group = lax.rem(z_hi + d, SIDE)
        wait_all(arriving[n])
        total = partial[5, rows_of(y * SIDE + group)]
        first_sum[2, n * ROWS : (n + 1) * ROWS] = (
            total + first_in[2, n, 0] + (first_in[2, n, 1] + first_in[2, n, 2])
        )
        if d:
            copies.append(
                send(
                    first_sum.at[2, n * ROWS : (n + 1) * ROWS],
                    second_in.at[2, d - 1],
                    around("z_hi", d),
                )
            )
    flush(len(pending) - len(copies))
    take_result(handed[1], 1)
    wait_all(copies)
    total = first_sum[2, 3 * ROWS : 4 * ROWS]
    solved[6] = total + second_in[2, 0] + (second_in[2, 1] + second_in[2, 2])
    first = give_result(solved.at[6], 0)
    take_result(first, 0)
    flush(len(pending))


def hand_over(first, second, third, root, out_first, out_second, out_third, out_root):
    out_first[...] = first[...]
    out_second[...] = second[...]
    out_third[...] = third[...]
    for p in range(2):
        out_root[:, p, :] = root[:, p * HALF : (p + 1) * HALF]


def local(*operands):
    f32, bf16 = jnp.float32, jnp.bfloat16
    rhs_rows = operands[0].shape[0]
    vmem = pl.BlockSpec(memory_space=pltpu.VMEM)
    smem = pl.BlockSpec(memory_space=pltpu.SMEM)
    whole = pl.BlockSpec(memory_space=pltpu.HBM)
    outputs = pl.pallas_call(
        solve_kernel,
        out_shape=[jax.ShapeDtypeStruct((rhs_rows, SPAN), f32)] * 4,
        in_specs=[whole] + [whole, whole, smem, smem] * 3 + [smem, whole, whole],
        out_specs=[vmem] * 4,
        scratch_shapes=[
            pltpu.VMEM((2 * ROWS, GROUPS * BLOCK), f32),
            pltpu.VMEM((3, RED, BLOCK, BLOCK), f32),
            pltpu.VMEM((3, RED, LINKS, BLOCK, BLOCK), f32),
            pltpu.VMEM((3, RED, 3 * BLOCK, BLOCK), bf16),
            pltpu.VMEM((3, RED, 3 * BLOCK, LINKS * BLOCK), bf16),
            pltpu.VMEM((3, SKELETONS[0], 2 * ROWS, BLOCK), f32),
            pltpu.VMEM((SKELETONS[0], 2 * ROWS, BLOCK), f32),
            pltpu.VMEM((SKELETONS[1], 2 * ROWS, BLOCK), f32),
            pltpu.VMEM((SKELETONS[2], 2 * ROWS, BLOCK), f32),
            pltpu.VMEM((2, 2 * ROWS, HALF), f32),
            pltpu.VMEM((3, HALF, SPAN), f32),
            pltpu.VMEM((3, HALF, SPAN), f32),
            pltpu.VMEM((3, SPAN, SPAN), bf16),
            pltpu.VMEM((3, SPAN, SPAN), bf16),
            pltpu.VMEM((2, ROWS, SPAN), f32),
            pltpu.VMEM((2, ROWS, SPAN), f32),
            pltpu.VMEM((ROWS, SPAN), f32),
            pltpu.VMEM((2, SIDE * ROWS, SPAN), f32),
            pltpu.VMEM((STEPS, TOTAL, SPAN), f32),
            pltpu.VMEM((STEPS, TOTAL, SPAN), f32),
            pltpu.VMEM((3, GROUPS - 1, ROWS, SPAN), f32),
            pltpu.VMEM((3, SIDE, SIDE, ROWS, SPAN), f32),
            pltpu.VMEM((3, SIDE * ROWS, SPAN), f32),
            pltpu.VMEM((3, SIDE, ROWS, SPAN), f32),
            pltpu.VMEM((7, ROWS, SPAN), f32),
            pltpu.VMEM((2, ROWS, HALF), f32),
            pltpu.SemaphoreType.DMA((MESSAGES,)),
            pltpu.SemaphoreType.DMA((MESSAGES,)),
            pltpu.SemaphoreType.DMA((10,)),
        ],
        compiler_params=pltpu.CompilerParams(
            collective_id=0, has_side_effects=True, vmem_limit_bytes=63 << 20
        ),
        name="solve",
    )(*operands[:13], operands[13].T, *operands[14:])
    shapes = [jax.ShapeDtypeStruct((rhs_rows, SPAN), f32)] * 3
    return pl.pallas_call(
        hand_over,
        out_shape=[*shapes, jax.ShapeDtypeStruct((rhs_rows, 2, HALF), f32)],
        in_specs=[vmem] * 4,
        out_specs=[vmem] * 4,
        name="hand_over",
    )(*outputs)


def solution(mesh):
    in_specs = (
        P("col", "leaf"),
        P("leaf", None, None),
        P("leaf", None, None, None),
        P("leaf", None),
        P("leaf", None),
        P("leaf", None, None),
        P("leaf", None, None, None),
        P("leaf", None),
        P("leaf", None),
        P("leaf", None, None),
        P("leaf", None, None, None),
        P("leaf", None),
        P("leaf", None),
        P(None, "leaf"),
        P(None, "leaf", "col"),
        P("leaf", "col"),
    )
    out_specs = (P("col", "leaf"), P("col", "leaf"), P("col", "leaf"), P("col", None, "leaf"))
    return jax.shard_map(local, mesh=mesh, in_specs=in_specs, out_specs=out_specs, check_vma=False)
```
